32 devices in a mesh: micro: 4 (over z), grid: 8 (over y, x, core).
Axes of the slice: x: 2, y: 2, z: 4, core: 2. Of those that a mesh axis runs over, the one named last changes fastest.
Arguments:
- orbitals: float32 [2, 32, 64, 16, 256], P(None, 'micro', None, 'grid'), may hold values from -14 to 14
- local_potential: float32 [32, 16, 256], P('micro', 'grid'), may hold values from -1 to 1
- projectors: float32 [2, 32, 16, 256], P(None, None, 'grid'), may hold values from -0.09375 to 0.09375
- strengths: float32 [2, 32], replicated, may hold values from 1 to 12
- material: int32 [32], replicated, may hold values from 0 to 1
- proj_kind: int32 [32], replicated, may hold values from 0 to 1
- point_cell: int32 [32], replicated, may hold values from 0 to 1999
- vector_now: float32 [2000], replicated, may hold values from -3 to 3
- vector_old: float32 [2000], replicated, may hold values from -3 to 3
Outputs:
- orbitals_out: float32 [2, 32, 64, 16, 256], P(None, 'micro', None, 'grid')
- vector_field: float32 [2000], replicated
The draws below stay inside these ranges and needn't reach their ends.
All inputs are finite; a program needn't handle non-finite values.
Results may differ from the reference program's by a relative error of at most 0.0003.
Values sent between devices are 32-bit elements; how exact they have to be, the bound alone decides.
A program may use at most 128 MiB of HBM per device.

```python
import math
import jax
import jax.numpy as jnp
from jax import lax

NX = 16
NY = 16
NZ = 16
ORB = 64
NPROJ = 32
KINDS = 2
POINTS = 32
MACRO_CELLS = 2000
STEPS = 2
ORDER = 4


def draw_orbitals(key, part):
    subkeys = jax.random.split(key, 3)
    cells = NY * NZ
    z_index = (jnp.arange(cells, dtype=jnp.int32) % NZ).astype(jnp.float32)
    wave_modes = jax.random.randint(subkeys[0], (POINTS, ORB, 1, 1), 1, NZ // 4 + 1).astype(jnp.float32)
    phases = jax.random.uniform(subkeys[1], (POINTS, ORB, 1, 1), minval=-math.pi, maxval=math.pi)
    angular_offset = 2.0 * math.pi * wave_modes * z_index / NZ + phases
    planes = jnp.arange(NX).astype(jnp.float32)
    growing_amplitude = (3.0 ** (planes / (NX - 1))).reshape(1, 1, NX, 1)
    large_scale_share = 0.6 * jnp.clip(jax.random.normal(subkeys[2], (2, POINTS, ORB, NX, cells)), -6.0, 6.0)
    scaling_coefficient = jnp.ones((POINTS, ORB, 1, 1), jnp.float32)
    oscillating_cosine = jnp.stack([jnp.cos(angular_offset), jnp.sin(angular_offset)])
    return (growing_amplitude * scaling_coefficient * (oscillating_cosine + large_scale_share)).astype(jnp.float32)


def with_ends(drawn, stream_key, low, top_value):
    shape = drawn.shape
    index_at = [jax.random.randint(jax.random.fold_in(stream_key, axis), (), 0, shape[axis]) for axis in range(len(shape))]
    drawn = drawn.at[tuple(index_at)].set(low)
    longest = shape.index(max(shape))
    index_at[longest] = (index_at[longest] + 1) % shape[longest]
    return drawn.at[tuple(index_at)].set(top_value)


def block_levels(stream_key, shape, cuts, low, largest):
    def one(dim, parts):
        steps = jax.random.uniform(jax.random.fold_in(jax.random.fold_in(stream_key, 6), dim), (parts,), jnp.float32, low / len(cuts), largest / len(cuts))
        return jnp.repeat(jnp.exp(steps), shape[dim] // parts).reshape((-1,) + (1,) * (len(shape) - dim - 1))

    gain = one(*cuts[0])
    for cut in cuts[1:]:
        gain = gain * one(*cut)
    return gain


def noise(stream_key, shape, width, reach, pieces=(), kind=jnp.bfloat16):
    values = jax.random.normal(stream_key, shape, jnp.float32) * width
    if len(pieces) > 0:
        values = block_levels(stream_key, shape, pieces, -0.22, 0.18) * values
    return jnp.clip(values, min=-reach, max=reach).astype(kind)


def setup_inputs(seed: int = 0) -> dict:
    keys = jax.random.split(jax.random.key(seed), 10)
    return {
        "orbitals": draw_orbitals(jax.random.fold_in(keys[9], 71), 0),
        "local_potential": jnp.clip(jax.random.uniform(keys[1], (POINTS, NX, NY * NZ), jnp.float32, -1.0, 1.0) * block_levels(keys[1], (POINTS, NX, NY * NZ), ((0, 4), (1, 8)), -0.4, 0.0), -1.0, 1.0),
        "projectors": noise(keys[2], (KINDS, NPROJ, NX, NY * NZ), (NX * NY * NZ) ** -0.5, 0.09375, ((2, 8),), jnp.float32),
        "strengths": jnp.clip(jnp.exp(jax.random.uniform(keys[3], (KINDS, NPROJ), jnp.float32, math.log(1.0), math.log(12.0))), 1.0, 12.0),
        "material": with_ends(jax.random.randint(keys[4], (POINTS,), 0, 2), jax.random.fold_in(keys[4], 1), 0, 1).astype(jnp.int32),
        "proj_kind": with_ends(jax.random.randint(keys[5], (POINTS,), 0, KINDS), jax.random.fold_in(keys[5], 1), 0, KINDS - 1).astype(jnp.int32),
        "point_cell": with_ends(jax.random.randint(keys[6], (POINTS,), 0, MACRO_CELLS), jax.random.fold_in(keys[6], 1), 0, MACRO_CELLS - 1).astype(jnp.int32),
        "vector_now": noise(keys[7], (MACRO_CELLS,), 0.5, 3.0, (), jnp.float32),
        "vector_old": noise(keys[8], (MACRO_CELLS,), 0.5, 3.0, (), jnp.float32),
    }


SPACING = 0.64
TIME_STEP = 0.05
COURANT = 0.9
COUPLING = 1.0
HIGHEST = lax.Precision.HIGHEST


def z_gradient(field):
    extent = field.shape
    blocks = field.reshape(extent[:-1] + (NY, NZ))
    change = jnp.roll(blocks, -1, len(extent)) - jnp.roll(blocks, 1, len(extent))
    return change.reshape(extent) / (2.0 * SPACING)


def neighbour_sums(field):
    extent = field.shape
    blocks = field.reshape(extent[:-1] + (NY, NZ))
    horizontal_direction = jnp.roll(blocks, 1, 3) + jnp.roll(blocks, -1, 3)
    along_y = jnp.roll(blocks, 1, 4) + jnp.roll(blocks, -1, 4)
    forward = jnp.roll(blocks, -1, 5)
    backward = jnp.roll(blocks, 1, 5)
    beside_all = (horizontal_direction + along_y + forward + backward).reshape(extent)
    field_gradient = (forward - backward).reshape(extent) / (2.0 * SPACING)
    return beside_all, field_gradient


def apply_hamiltonian(field, field_at, potential, beta_flat, weights):
    beside_all, field_gradient = neighbour_sums(field)
    diagonal = 3.0 / SPACING ** 2 + 0.5 * field_at * field_at + potential
    kinetic = diagonal * field - beside_all / (2.0 * SPACING ** 2)
    drift = jnp.stack([field_gradient[1], -field_gradient[0]]) * field_at
    flattened_rows = field.reshape(-1, beta_flat.shape[1])
    intersection = jnp.dot(flattened_rows, beta_flat.T, precision=HIGHEST)
    intersection = intersection.reshape(field.shape[:3] + (-1,)) * weights[None, :, None, :]
    nonlocal_part = jnp.dot(intersection.reshape(flattened_rows.shape[0], -1), beta_flat, precision=HIGHEST)
    return kinetic + drift + nonlocal_part.reshape(field.shape)


def point_current(field, field_at, occupied):
    field_gradient = z_gradient(field)
    flow = field[0] * field_gradient[1] - field[1] * field_gradient[0]
    density = field[0] * field[0] + field[1] * field[1]
    per_orbital = jnp.sum(flow + field_at * density, axis=(2, 3))
    return jnp.sum(per_orbital * occupied, axis=1) * (2.0 / (ORB * NX * NY * NZ))


def reference(orbitals, local_potential, projectors, strengths, material, proj_kind, point_cell, vector_now, vector_old):
    beta_flat = projectors.reshape(KINDS * NPROJ, NX * NY * NZ)
    kind_onehot = (proj_kind[:, None] == jnp.arange(KINDS, dtype=jnp.int32)[None, :]).astype(jnp.float32)
    weights = (kind_onehot[:, :, None] * strengths[None]).reshape(POINTS, KINDS * NPROJ)
    orbital_ids = jnp.arange(ORB, dtype=jnp.int32)
    occupied = ((orbital_ids[None, :] < ORB // 2) | (material[:, None] == 1)).astype(jnp.float32)
    potential = local_potential[:, None]
    macro_ids = jnp.arange(MACRO_CELLS, dtype=jnp.int32)
    placement = (point_cell[:, None] == macro_ids[None, :]).astype(jnp.float32)
    field = orbitals
    present = vector_now
    previous = vector_old
    for step_index in range(STEPS):
        field_at = present[point_cell].reshape(POINTS, 1, 1, 1)
        summed = field
        taylor_term = field
        for degree in range(1, ORDER + 1):
            applied = apply_hamiltonian(taylor_term, field_at, potential, beta_flat, weights)
            taylor_term = (TIME_STEP / degree) * jnp.stack([applied[1], -applied[0]])
            summed = summed + taylor_term
        field = summed
        currents = point_current(field, field_at, occupied)
        accumulate_current = jnp.dot(currents, placement, precision=HIGHEST)
        extended_with_zeros = jnp.pad(present, 1)
        curvature = extended_with_zeros[2:] + extended_with_zeros[:-2] - 2.0 * present
        following = 2.0 * present - previous + COURANT ** 2 * curvature - COUPLING * accumulate_current
        previous = present
        present = following
    return field * occupied[None, :, :, None, None], present
```

```python
import functools

import jax
import jax.numpy as jnp
from jax import lax
from jax.experimental import pallas as pl
from jax.experimental.pallas import tpu as pltpu
from jax.sharding import PartitionSpec as P

NZ = 16
STEPS = 2
ORDER = 4
LANES = 128
GROUPS = 2

SPACING = 0.64
TIME_STEP = 0.05
COURANT = 0.9
COUPLING = 1.0
F32 = jnp.float32
BF16 = jnp.bfloat16


def halves(value):
    high = value.astype(BF16)
    return high, (value - high.astype(F32)).astype(BF16)


def macro_update(present, previous, deposit, macro):
    high, lanes = present.shape
    lane = lax.broadcasted_iota(jnp.int32, present.shape, 1)
    flat = lax.broadcasted_iota(jnp.int32, present.shape, 0) * lanes + lane
    ahead = pltpu.roll(present, lanes - 1, 1)
    ahead = jnp.where(lane == lanes - 1, pltpu.roll(ahead, high - 1, 0), ahead)
    behind = pltpu.roll(present, 1, 1)
    behind = jnp.where(lane == 0, pltpu.roll(behind, 1, 0), behind)
    curvature = ahead + behind - 2.0 * present
    following = 2.0 * present - previous + COURANT**2 * curvature - COUPLING * deposit
    return jnp.where(flat < macro, following, 0.0)


def kernel(
    norm, macro, share, grid, layers, mine, own,
    material_ref, kind_ref, cell_ref, strength_ref, projector_ref, potential_ref, now_ref, old_ref, field_ref,
    out_ref, vector_ref,
    terms_ref, land_ref, parts_ref, packed_ref, side_ref, fore_ref, back_ref, diag_ref, weight_ref, previous_ref,
    row_ref, rows_ref, all_ref,
    in_send, in_recv, side_send, side_recv, out_send, out_recv, row_send, row_recv, all_send, all_recv, own_sem,
):
    _, groups, slots, cells, lanes = terms_ref.shape
    slots = slots - 2
    kinds, nproj = strength_ref.shape
    points = potential_ref.shape[0]
    per = potential_ref.shape[1]
    wide = cells // lanes
    orbs = own // groups
    blocks = lanes // (2 * orbs)
    here = lax.axis_index("grid")
    layer = lax.axis_index("micro")
    my_point = lax.div(here, share)
    first_orbital = lax.rem(here, share) * own
    me = layer * points + my_point
    limit = jnp.where(material_ref[me] == 1, share * own, share * own // 2) - first_orbital
    my_cell, my_kind = cell_ref[me], kind_ref[me]
    barrier = pltpu.get_barrier_semaphore()
    piece = orbs * per

    def beside_me(distance):
        return lax.rem(here + distance, grid)

    def above_me(distance):
        return lax.rem(layer + distance, layers)

    def remote(source, target, sent, received, device):
        return pltpu.make_async_remote_copy(
            src_ref=source, dst_ref=target, send_sem=sent, recv_sem=received,
            device_id=device, device_id_type=pl.DeviceIdType.MESH,
        )

    def field_part(ref, group, device):
        first = (lax.rem(device, share) * own + group * orbs) * per
        return ref.at[:, lax.div(device, share), pl.ds(pl.multiple_of(first, 8), piece), :]

    def side_copy(distance, owner):
        other = beside_me(distance)
        return remote(
            packed_ref.at[other], side_ref.at[owner], side_send.at[distance], side_recv.at[owner], (layer, other)
        )

    def in_copy(group, distance, owner):
        other = beside_me(distance)
        return remote(
            field_part(field_ref, group, other), land_ref.at[group, owner],
            in_send.at[group, distance], in_recv.at[group, owner], (layer, other),
        )

    def out_copy(group, distance, owner):
        other = beside_me(distance)
        return remote(
            land_ref.at[group, other], field_part(out_ref, group, owner),
            out_send.at[group, distance], out_recv.at[group, owner], (layer, other),
        )

    def own_side():
        return pltpu.make_async_copy(packed_ref.at[here], side_ref.at[here], own_sem.at[0])

    def own_in(group):
        return pltpu.make_async_copy(field_part(field_ref, group, here), land_ref.at[group, here], own_sem.at[1 + group])

    def own_out(group):
        return pltpu.make_async_copy(
            land_ref.at[group, here], field_part(out_ref, group, here), own_sem.at[1 + groups + group]
        )

    @pl.loop(1, grid)
    def _(distance):
        pl.semaphore_signal(
            barrier, inc=1, device_id=(layer, beside_me(distance)), device_id_type=pl.DeviceIdType.MESH
        )

    @pl.loop(1, layers)
    def _(distance):
        pl.semaphore_signal(
            barrier, inc=1, device_id=(above_me(distance), here), device_id_type=pl.DeviceIdType.MESH
        )

    for group in range(groups):
        own_in(group).start()
    for target in range(grid):
        kind = kind_ref[layer * points + target // share]
        chosen = jnp.zeros(projector_ref.shape[1:], F32)
        for number in range(kinds):
            chosen = jnp.where(kind == number, projector_ref[number], chosen)
        packed_ref[target, :nproj * per] = chosen
        packed_ref[target, nproj * per:nproj * per + per] = potential_ref[target // share]
    own_side().start()
    vector_ref[...] = now_ref[...]
    previous_ref[...] = old_ref[...]
    pl.semaphore_wait(barrier, grid + layers - 2)

    @pl.loop(1, grid)
    def _(distance):
        side_copy(distance, here).start()

    for group in range(groups):
        @pl.loop(1, grid)
        def _(distance):
            in_copy(group, distance, here).start()

    lane = lax.broadcasted_iota(jnp.int32, (1, lanes), 1)
    real = lane < lanes // 2
    block_of = lax.rem(lane, lanes // 2) // orbs
    orbital_of = lax.rem(lane, orbs)
    sign = jnp.where(real, 1.0, -1.0).astype(F32)

    def turn(value, count):
        if blocks == 1:
            return value
        count = count % blocks
        inside = pltpu.roll(value, count * orbs, 1)
        around = pltpu.roll(value, lanes // 2 + count * orbs, 1)
        return jnp.where(lax.rem(lax.broadcasted_iota(jnp.int32, value.shape, 1), lanes // 2) >= count * orbs, inside, around)

    weight = jnp.where(my_kind == 0, strength_ref[0:1, :], 0.0)
    for number in range(1, kinds):
        weight = weight + jnp.where(my_kind == number, strength_ref[number:number + 1, :], 0.0)
    weight = jnp.broadcast_to(weight * (2.0 * SPACING**2), (nproj, nproj))
    eye = lax.broadcasted_iota(jnp.int32, (nproj, nproj), 0) == lax.broadcasted_iota(jnp.int32, (nproj, nproj), 1)
    weight_ref[...] = jnp.broadcast_to(jnp.sum(jnp.where(eye, weight, 0.0), axis=1, keepdims=True), (nproj, lanes))

    own_side().wait()

    @pl.loop(1, grid)
    def _(distance):
        side_copy(distance, here).wait_send()
        side_copy(distance, beside_me(distance)).wait_recv()

    def prepare(slot, carry):
        for half in range(wide):
            here_lanes = slice(half * lanes, (half + 1) * lanes)
            level = []
            for block in range(blocks):
                x = block * slots + slot
                owner, plane = lax.div(x, mine), lax.rem(x, mine)
                row = half * mine + plane
                beta = side_ref[owner, pl.ds(row, nproj, stride=per), :]
                high, low = halves(beta)
                top = block * 2 * nproj
                fore_ref[slot, top:top + nproj, here_lanes] = high
                fore_ref[slot, top + nproj:top + 2 * nproj, here_lanes] = low
                high, low = high.astype(F32), low.astype(F32)
                tall = jnp.concatenate([high, low, high, low], axis=0)
                back_ref[slot, here_lanes, block * lanes:(block + 1) * lanes] = tall.T.astype(BF16)
                level.append(jnp.broadcast_to(side_ref[owner, pl.ds(nproj * per + row, 1), :], (orbs, lanes)))
            diag_ref[slot, here_lanes, :] = jnp.concatenate(level * 2, axis=0).T * (2.0 * SPACING**2)
        return carry

    lax.fori_loop(0, slots, prepare, 0)

    def keep(term, group, slot, rows, value):
        terms_ref[term, group, slot + 1, rows, :] = value

    def edges(term, group):
        def one(step, carry):
            rows = pl.ds(pl.multiple_of(step * NZ, NZ), NZ)
            terms_ref[term, group, 0, rows, :] = turn(terms_ref[term, group, slots, rows, :], 1)
            terms_ref[term, group, slots + 1, rows, :] = turn(terms_ref[term, group, 1, rows, :], blocks - 1)
            return carry

        lax.fori_loop(0, cells // NZ, one, 0, unroll=4)

    def setup(group):
        def one(slot, carry):
            for half in range(wide):
                pieces = []
                for part in range(2):
                    for block in range(blocks):
                        x = block * slots + slot
                        owner, plane = lax.div(x, mine), lax.rem(x, mine)
                        pieces.append(land_ref[group, owner, part, pl.ds(half * mine + plane, orbs, stride=per), :])
                value = jnp.concatenate(pieces, axis=0).T
                rows = slice(half * lanes, (half + 1) * lanes)
                terms_ref[0, group, slot + 1, rows, :] = value
                high, low = halves(value)
                parts_ref[group, slot, rows, :lanes] = high
                parts_ref[group, slot, rows, lanes:] = low
            return carry

        lax.fori_loop(0, slots, one, 0)
        edges(0, group)

    def finish(group):
        def one(slot, carry):
            for half in range(wide):
                value = terms_ref[0, group, slot + 1, half * lanes:(half + 1) * lanes, :]
                occupied = jnp.where(orbital_of + group * orbs < limit, 1.0, 0.0)
                value = (value * occupied).T
                for part in range(2):
                    for block in range(blocks):
                        x = block * slots + slot
                        owner, plane = lax.div(x, mine), lax.rem(x, mine)
                        top = (part * blocks + block) * orbs
                        land_ref[group, owner, part, pl.ds(half * mine + plane, orbs, stride=per), :] = value[top:top + orbs]
            return carry

        lax.fori_loop(0, slots, one, 0)

    def contract(group):
        total = jnp.zeros((blocks * 2 * nproj, 2 * lanes), F32)
        for slot in range(slots):
            total = total + jnp.dot(fore_ref[slot], parts_ref[group, slot], preferred_element_type=F32)
        total = total[:, :lanes] + total[:, lanes:]
        c = jnp.zeros((nproj, lanes), F32)
        for block in range(blocks):
            top = block * 2 * nproj
            both = total[top:top + nproj] + total[top + nproj:top + 2 * nproj]
            c = c + jnp.where(block_of == block, both, 0.0)
        summed = c
        for count in range(1, blocks):
            summed = summed + turn(c, count)
        summed = summed * weight_ref[...]
        high, low = halves(summed)
        tall = jnp.concatenate([high, high, low, low], axis=0).astype(F32)
        return jnp.concatenate([jnp.where(block_of == block, tall, 0.0) for block in range(blocks)], axis=0).astype(BF16)

    def degree_pass(group, degree, a, last_step, acc):
        scale = TIME_STEP / degree
        right = contract(group)
        swap_scale = sign * (scale / (2.0 * SPACING**2))
        drift_scale = a * (scale / (2.0 * SPACING))
        base = 6.0 + (SPACING * SPACING) * a * a
        source = degree - 1
        final = degree == ORDER
        target = 0 if final else degree

        def one(slot, acc):
            nonlocal_part = jnp.dot(back_ref[slot], right, preferred_element_type=F32)
            for y in range(cells // NZ):
                rows = slice(y * NZ, (y + 1) * NZ)
                up = (y + 1) % (cells // NZ) * NZ
                down = (y - 1) % (cells // NZ) * NZ
                value = terms_ref[source, group, slot + 1, rows, :]
                ahead, behind = pltpu.roll(value, NZ - 1, 0), pltpu.roll(value, 1, 0)
                beside = (ahead + behind) + (
                    terms_ref[source, group, slot + 1, up:up + NZ, :] + terms_ref[source, group, slot + 1, down:down + NZ, :]
                ) + (terms_ref[source, group, slot, rows, :] + terms_ref[source, group, slot + 2, rows, :])
                level = (diag_ref[slot, rows, :] + base) * value - beside + nonlocal_part[rows]
                new = swap_scale * pltpu.roll(level, lanes // 2, 1) - drift_scale * (ahead - behind)
                if final:
                    new = new + value
                    for term in range(source):
                        new = new + terms_ref[term, group, slot + 1, rows, :]
                    flow, density = acc
                    slope = pltpu.roll(new, NZ - 1, 0) - pltpu.roll(new, 1, 0)
                    acc = (flow + new * pltpu.roll(slope, lanes // 2, 1), density + new * new)
                terms_ref[target, group, slot + 1, rows, :] = new
                high, low = halves(new)
                parts_ref[group, slot, rows, :lanes] = high
                parts_ref[group, slot, rows, lanes:] = low
            return acc

        acc = lax.fori_loop(0, slots, one, acc)
        edges(target, group)
        return acc

    def advance_group(step, group, a):
        @pl.when(step == 0)
        def _():
            own_in(group).wait()

            @pl.loop(1, grid)
            def _(distance):
                in_copy(group, distance, here).wait_send()
                in_copy(group, distance, beside_me(distance)).wait_recv()

            setup(group)

        acc = (jnp.zeros((NZ, lanes), F32), jnp.zeros((NZ, lanes), F32))
        for degree in range(1, ORDER + 1):
            acc = degree_pass(group, degree, a, False, acc)
        flow, density = acc
        occupied = jnp.where(orbital_of + group * orbs < limit, 1.0, 0.0)

        @pl.when(step == STEPS - 1)
        def _():
            finish(group)

            @pl.loop(1, grid)
            def _(distance):
                out_copy(group, distance, here).start()

            own_out(group).start()

        return jnp.sum(flow * (sign * (0.5 / SPACING)) * occupied + a * density * occupied)

    flat = (
        lax.broadcasted_iota(jnp.int32, now_ref.shape, 0) * now_ref.shape[1]
        + lax.broadcasted_iota(jnp.int32, now_ref.shape, 1)
    )

    def row_copy(step, distance, owner):
        other = beside_me(distance)
        return remote(
            row_ref.at[step], rows_ref.at[step, owner], row_send.at[step, distance], row_recv.at[step, owner], (layer, other)
        )

    def all_copy(step, distance, owner):
        return remote(
            rows_ref.at[step], all_ref.at[step, owner],
            all_send.at[step, distance], all_recv.at[step, owner], (above_me(distance), here),
        )

    def advance(step, carry):
        a = jnp.sum(jnp.where(flat == my_cell, vector_ref[...], 0.0))
        total = lax.fori_loop(0, groups, lambda group, total: total + advance_group(step, group, a), jnp.float32(0.0))
        row_ref[step] = jnp.full((1, LANES), total * norm, F32)

        @pl.loop(1, grid)
        def _(distance):
            row_copy(step, distance, here).start()

        rows_ref[step, here] = row_ref[step]

        @pl.loop(1, grid)
        def _(distance):
            row_copy(step, distance, here).wait_send()
            row_copy(step, distance, beside_me(distance)).wait_recv()

        @pl.loop(1, layers)
        def _(distance):
            all_copy(step, distance, layer).start()

        all_ref[step, layer] = rows_ref[step]

        @pl.loop(1, layers)
        def _(distance):
            all_copy(step, distance, layer).wait_send()
            all_copy(step, distance, above_me(distance)).wait_recv()

        deposit = jnp.zeros(flat.shape, F32)
        for storey in range(layers):
            for member in range(grid):
                cell = cell_ref[storey * points + member // share]
                deposit = deposit + jnp.where(flat == cell, all_ref[step, storey, member], 0.0)
        present = vector_ref[...]
        vector_ref[...] = macro_update(present, previous_ref[...], deposit, macro)
        previous_ref[...] = present
        return carry

    lax.fori_loop(0, STEPS, advance, 0)
    for group in range(groups):
        own_out(group).wait()

        @pl.loop(1, grid)
        def _(distance):
            out_copy(group, distance, here).wait_send()
            out_copy(group, distance, beside_me(distance)).wait_recv()


def propagate(materials, kinds, owners, strengths, projectors, potential, now, old, field, norm, macro, share, grid, layers, mine, own):
    points, per, lanes = potential.shape
    cells = per // mine * lanes
    planes = grid * mine
    orbs = own // GROUPS
    blocks = lanes // (2 * orbs)
    slots = planes // blocks
    nproj = strengths.shape[1]
    rows = nproj * per
    tall = rows + -(-per // 8) * 8
    vmem = pl.BlockSpec(memory_space=pltpu.VMEM)
    smem = pl.BlockSpec(memory_space=pltpu.SMEM)
    anywhere = pl.BlockSpec(memory_space=pl.ANY)
    dma = lambda *shape: pltpu.SemaphoreType.DMA(shape)
    return pl.pallas_call(
        functools.partial(kernel, norm, macro, share, grid, layers, mine, own),
        out_shape=(
            jax.ShapeDtypeStruct(field.shape, F32),
            jax.ShapeDtypeStruct(now.shape, F32),
        ),
        in_specs=[smem] * 3 + [vmem] * 5 + [anywhere],
        out_specs=(anywhere, vmem),
        scratch_shapes=[
            pltpu.VMEM((ORDER, GROUPS, slots + 2, cells, lanes), F32),
            pltpu.VMEM((GROUPS, grid, 2, orbs * per, lanes), F32),
            pltpu.VMEM((GROUPS, slots, cells, 2 * lanes), BF16),
            pltpu.VMEM((grid, tall, lanes), F32),
            pltpu.VMEM((grid, tall, lanes), F32),
            pltpu.VMEM((slots, blocks * 2 * nproj, cells), BF16),
            pltpu.VMEM((slots, cells, blocks * lanes), BF16),
            pltpu.VMEM((slots, cells, lanes), F32),
            pltpu.VMEM((nproj, lanes), F32),
            pltpu.VMEM(now.shape, F32),
            pltpu.VMEM((STEPS, 1, LANES), F32),
            pltpu.VMEM((STEPS, grid, 1, LANES), F32),
            pltpu.VMEM((STEPS, layers, grid, 1, LANES), F32),
            dma(GROUPS, grid), dma(GROUPS, grid),
            dma(grid), dma(grid),
            dma(GROUPS, grid), dma(GROUPS, grid),
            dma(STEPS, grid), dma(STEPS, grid),
            dma(STEPS, layers), dma(STEPS, layers),
            dma(1 + 2 * GROUPS),
        ],
        compiler_params=pltpu.CompilerParams(
            vmem_limit_bytes=48 * 1024 * 1024, collective_id=0, has_side_effects=True
        ),
        name="propagate",
    )(materials, kinds, owners, strengths, projectors, potential, now, old, field)


def rows_of(array, lanes=LANES):
    lead, (planes, cells) = array.shape[:-2], array.shape[-2:]
    array = array.reshape(lead + (planes, cells // lanes, lanes))
    return jnp.swapaxes(array, -3, -2).reshape(lead + (planes * cells // lanes, lanes))


def local(
    orbitals, local_potential, projectors, strengths, material, proj_kind, point_cell,
    vector_now, vector_old, grid, layers,
):
    _, points, orb, mine, cells = orbitals.shape
    assert grid % points == 0 and orb % (grid // points) == 0
    share = grid // points
    own = orb // share
    wide = cells // LANES
    per = wide * mine
    kinds, nproj = strengths.shape
    macro = vector_now.shape[0]
    padded = (macro // 1024 + 1) * 1024
    lay = lambda vector: jnp.pad(vector, (0, padded - macro)).reshape(-1, LANES)
    field, vector = propagate(
        material, proj_kind, point_cell, strengths,
        rows_of(projectors).reshape(kinds, nproj * per, LANES),
        rows_of(local_potential),
        lay(vector_now), lay(vector_old),
        rows_of(orbitals).reshape(2, points, orb * per, LANES),
        2.0 / (orb * grid * mine * cells), macro, share, grid, layers, mine, own,
    )
    field = jnp.swapaxes(field.reshape(2, points, orb, wide, mine, LANES), -3, -2).reshape(orbitals.shape)
    return field, vector.reshape(-1)[:macro]


def solution(mesh):
    in_specs = (
        P(None, "micro", None, "grid", None),
        P("micro", "grid", None),
        P(None, None, "grid", None),
        P(),
        P(),
        P(),
        P(),
        P(),
        P(),
    )
    out_specs = (P(None, "micro", None, "grid", None), P())
    body = functools.partial(local, grid=mesh.shape["grid"], layers=mesh.shape["micro"])
    return jax.shard_map(body, mesh=mesh, in_specs=in_specs, out_specs=out_specs, check_vma=False)
```

```python
import functools

import jax
import jax.numpy as jnp
from jax import lax
from jax.experimental import pallas as pl
from jax.experimental.pallas import tpu as pltpu
from jax.sharding import PartitionSpec as P

NZ = 16
STEPS = 2
ORDER = 4
LANES = 128
GROUPS = 4

SPACING = 0.64
TIME_STEP = 0.05
COURANT = 0.9
COUPLING = 1.0
F32 = jnp.float32
BF16 = jnp.bfloat16


def halves(value):
    high = value.astype(BF16)
    return high, (value - high.astype(F32)).astype(BF16)


def macro_update(present, previous, deposit, macro):
    high, lanes = present.shape
    lane = lax.broadcasted_iota(jnp.int32, present.shape, 1)
    flat = lax.broadcasted_iota(jnp.int32, present.shape, 0) * lanes + lane
    ahead = pltpu.roll(present, lanes - 1, 1)
    ahead = jnp.where(lane == lanes - 1, pltpu.roll(ahead, high - 1, 0), ahead)
    behind = pltpu.roll(present, 1, 1)
    behind = jnp.where(lane == 0, pltpu.roll(behind, 1, 0), behind)
    curvature = ahead + behind - 2.0 * present
    following = 2.0 * present - previous + COURANT**2 * curvature - COUPLING * deposit
    return jnp.where(flat < macro, following, 0.0)


def kernel(
    norm, macro, share, grid, layers, mine, own,
    material_in, kind_in, cell_in, strength_in, projector_in, potential_in, field_ref, now_ref, old_ref,
    out_ref, vector_ref,
    material_ref, kind_ref, cell_ref, strength_ref, projector_ref, potential_ref,
    terms_ref, land_ref, parts_ref, total_ref, packed_ref, side_ref, fore_ref, back_ref, diag_ref, level_ref, weight_ref,
    previous_ref, row_ref, rows_ref, flow_ref,
    in_send, in_recv, side_send, side_recv, out_send, out_recv, row_send, row_recv, load_sem,
):
    _, groups, slots, cells, lanes = terms_ref.shape
    slots = slots - 2
    kinds, nproj = strength_ref.shape
    points, per, _ = potential_ref.shape
    wide = cells // lanes
    orbs = own // groups
    blocks = lanes // (2 * orbs)
    here = lax.axis_index("grid")
    layer = lax.axis_index("micro")
    me = layer * points + lax.div(here, share)
    piece = orbs * per
    barrier = pltpu.get_barrier_semaphore()

    loads = [
        pltpu.make_async_copy(source, target, load_sem.at[number])
        for number, (source, target) in enumerate((
            (material_in, material_ref), (kind_in, kind_ref), (cell_in, cell_ref),
            (strength_in, strength_ref), (projector_in, projector_ref), (potential_in, potential_ref),
        ))
    ]

    def partner(mask):
        other, bit = 0, 1
        while bit < grid:
            own_bit = lax.rem(lax.div(here, bit), 2)
            other = other + (1 - own_bit if mask & bit else own_bit) * bit
            bit *= 2
        return other

    partners = {mask: partner(mask) for mask in range(1, grid)}
    core = lax.rem(here, 2)

    def ordered():
        chips = list(range(1, grid // 2))
        swapped = list(chips)
        if len(chips) >= 2:
            swapped[0], swapped[1] = chips[1], chips[0]
        for first, second in zip(chips, swapped):
            for bit in range(2):
                one, two = 2 * first + bit, 2 * second + bit
                yield one, two
        yield 1, 1

    order = []
    for one, two in ordered():
        order.append(partners[one] if one == two else partners[one] + core * (partners[two] - partners[one]))

    def storey(distance):
        return lax.rem(layer + distance, layers)

    def remote(source, target, sent, received, device):
        return pltpu.make_async_remote_copy(
            src_ref=source, dst_ref=target, send_sem=sent, recv_sem=received,
            device_id=device, device_id_type=pl.DeviceIdType.MESH,
        )

    def field_part(ref, group, device):
        first = (lax.rem(device, share) * own + group * orbs) * per
        return ref.at[:, lax.div(device, share), pl.ds(pl.multiple_of(first, 8), piece), :]

    def all_bytes(ref, sem):
        pltpu.make_async_copy(ref, ref, sem).wait()

    def signal(device):
        pl.semaphore_signal(barrier, inc=1, device_id=device, device_id_type=pl.DeviceIdType.MESH)

    for copy in loads:
        copy.start()
    for distance in range(layers):
        if distance > 0:
            signal((storey(distance), here))
        for other in partners.values():
            signal((storey(distance), other))

    def own_in(group):
        return pltpu.make_async_copy(field_part(field_ref, group, here), land_ref.at[group, here], in_recv.at[group])

    def own_out(group):
        return pltpu.make_async_copy(land_ref.at[group, here], field_part(out_ref, group, here), out_recv.at[group])

    def own_side():
        return pltpu.make_async_copy(packed_ref.at[here], side_ref.at[here], side_recv)

    for group in range(groups):
        own_in(group).start()
    for copy in loads:
        copy.wait()
    limit = jnp.where(material_ref[me] == 1, share * own, share * own // 2) - lax.rem(here, share) * own
    my_cell, my_kind = cell_ref[me], kind_ref[me]
    for target in range(grid):
        kind = kind_ref[layer * points + target // share]
        chosen = jnp.zeros(projector_ref.shape[1:], F32)
        for number in range(kinds):
            chosen = jnp.where(kind == number, projector_ref[number], chosen)
        packed_ref[target, :nproj * per] = chosen
        packed_ref[target, nproj * per:nproj * per + per] = potential_ref[target // share]
        spare = packed_ref.shape[1] - nproj * per - per
        if spare:
            packed_ref[target, nproj * per + per:] = jnp.zeros((spare, lanes), F32)
    own_side().start()
    pl.semaphore_wait(barrier, grid * layers - 1)
    for other in order:
        remote(packed_ref.at[other], side_ref.at[here], side_send, side_recv, (layer, other)).start()
    for group in range(groups):
        for other in order:
            remote(
                field_part(field_ref, group, other), land_ref.at[group, here],
                in_send.at[group], in_recv.at[group], (layer, other),
            ).start()

    vector_ref[...] = now_ref[...]
    previous_ref[...] = old_ref[...]
    lane = lax.broadcasted_iota(jnp.int32, (1, lanes), 1)
    block_of = lax.rem(lane, lanes // 2) // orbs
    orbital_of = lax.rem(lane, orbs)
    sign = jnp.where(lane < lanes // 2, 1.0, -1.0).astype(F32)
    place = lax.rem(lax.broadcasted_iota(jnp.int32, (NZ, lanes), 1), lanes // 2)

    def turn(value, count):
        if blocks == 1:
            return value
        shift = count % blocks * orbs
        mask = place[:value.shape[0]] >= shift
        return jnp.where(mask, pltpu.roll(value, shift, 1), pltpu.roll(value, lanes // 2 + shift, 1))

    weight = jnp.where(my_kind == 0, strength_ref[0:1, :], 0.0)
    for number in range(1, kinds):
        weight = weight + jnp.where(my_kind == number, strength_ref[number:number + 1, :], 0.0)
    weight = jnp.broadcast_to(weight * (2.0 * SPACING**2), (nproj, nproj))
    eye = lax.broadcasted_iota(jnp.int32, (nproj, nproj), 0) == lax.broadcasted_iota(jnp.int32, (nproj, nproj), 1)
    weight_ref[...] = jnp.broadcast_to(jnp.sum(jnp.where(eye, weight, 0.0), axis=1, keepdims=True), (nproj, lanes))

    all_bytes(side_ref, side_recv)

    def prepare(slot, carry):
        for half in range(wide):
            here_lanes = slice(half * lanes, (half + 1) * lanes)
            level = []
            for block in range(blocks):
                x = block * slots + slot
                owner, plane = lax.div(x, mine), lax.rem(x, mine)
                row = half * mine + plane
                beta = side_ref[owner, pl.ds(row, nproj, stride=per), :]
                high, low = halves(beta)
                top = block * 2 * nproj
                fore_ref[slot, top:top + nproj, here_lanes] = high
                fore_ref[slot, top + nproj:top + 2 * nproj, here_lanes] = low
                high, low = high.astype(F32), low.astype(F32)
                tall = jnp.concatenate([high, low, high, low], axis=0)
                back_ref[slot, here_lanes, block * lanes:(block + 1) * lanes] = tall.T.astype(BF16)
                level.append(jnp.broadcast_to(side_ref[owner, pl.ds(nproj * per + row, 1), :], (orbs, lanes)))
            diag_ref[slot, here_lanes, :] = jnp.concatenate(level * 2, axis=0).T * (2.0 * SPACING**2)
        return carry

    lax.fori_loop(0, slots, prepare, 0)

    def place_of(block, slot):
        x = block * slots + slot
        return lax.div(x, mine), lax.rem(x, mine)

    def store(term, group, slot, rows, value):
        terms_ref[term, group, slot + 1, rows, :] = value
        if slot == 0:
            terms_ref[term, group, slots + 1, rows, :] = turn(value, blocks - 1)
        if slot == slots - 1:
            terms_ref[term, group, 0, rows, :] = turn(value, 1)

    def setup(group):
        for slot in range(slots):
            for half in range(wide):
                pieces = []
                for part in range(2):
                    for block in range(blocks):
                        owner, plane = divmod(block * slots + slot, mine)
                        pieces.append(land_ref[group, owner, part, pl.ds(half * mine + plane, orbs, stride=per), :])
                value = jnp.concatenate(pieces, axis=0).T
                for y in range(lanes // NZ):
                    top = half * lanes + y * NZ
                    store(0, group, slot, slice(top, top + NZ), value[y * NZ:(y + 1) * NZ])

    def begin(group):
        total = jnp.zeros((blocks * 2 * nproj, 2 * lanes), F32)
        for slot in range(slots):
            high, low = halves(terms_ref[0, group, slot + 1])
            pieces = jnp.concatenate([high, low], axis=1)
            total = total + jnp.dot(fore_ref[slot], pieces, preferred_element_type=F32)
        total_ref[group] = total[:, :lanes] + total[:, lanes:]

    def finish(group):
        occupied = jnp.where(orbital_of + group * orbs < limit, 1.0, 0.0)
        for slot in range(slots):
            for half in range(wide):
                value = terms_ref[0, group, slot + 1, half * lanes:(half + 1) * lanes, :]
                value = (value * occupied).T
                for part in range(2):
                    for block in range(blocks):
                        owner, plane = divmod(block * slots + slot, mine)
                        top = (part * blocks + block) * orbs
                        land_ref[group, owner, part, pl.ds(half * mine + plane, orbs, stride=per), :] = value[top:top + orbs]

    def spread(total):
        c = jnp.zeros((nproj, lanes), F32)
        for block in range(blocks):
            top = block * 2 * nproj
            both = total[top:top + nproj] + total[top + nproj:top + 2 * nproj]
            c = c + jnp.where(block_of == block, both, 0.0)
        summed = c
        for count in range(1, blocks):
            summed = summed + jnp.concatenate([turn(c[:NZ], count), turn(c[NZ:], count)], axis=0)
        summed = summed * weight_ref[...]
        high, low = halves(summed)
        tall = jnp.concatenate([high, high, low, low], axis=0).astype(F32)
        return jnp.concatenate([jnp.where(block_of == block, tall, 0.0) for block in range(blocks)], axis=0).astype(BF16)

    def degrees(group, a):
        flow, density = jnp.zeros((NZ, lanes), F32), jnp.zeros((NZ, lanes), F32)
        total = total_ref[group]
        for degree in range(1, ORDER + 1):
            scale = TIME_STEP / degree
            right = spread(total)
            swap_scale = sign * (scale / (2.0 * SPACING**2))
            drift_scale = a * (scale / (2.0 * SPACING))
            source = degree - 1
            final = degree == ORDER
            for slot in range(slots):
                nonlocal_part = jnp.dot(back_ref[slot], right, preferred_element_type=F32)
                for y in range(cells // NZ):
                    rows = slice(y * NZ, (y + 1) * NZ)
                    up = (y + 1) % (cells // NZ) * NZ
                    down = (y - 1) % (cells // NZ) * NZ
                    value = terms_ref[source, group, slot + 1, rows, :]
                    ahead, behind = pltpu.roll(value, NZ - 1, 0), pltpu.roll(value, 1, 0)
                    beside = (ahead + behind) + (
                        terms_ref[source, group, slot + 1, up:up + NZ, :]
                        + terms_ref[source, group, slot + 1, down:down + NZ, :]
                    ) + (terms_ref[source, group, slot, rows, :] + terms_ref[source, group, slot + 2, rows, :])
                    level = level_ref[slot, rows, :] * value - beside + nonlocal_part[rows]
                    new = swap_scale * pltpu.roll(level, lanes // 2, 1) - drift_scale * (ahead - behind)
                    if final:
                        new = new + value
                        for term in range(source):
                            new = new + terms_ref[term, group, slot + 1, rows, :]
                        slope = pltpu.roll(new, NZ - 1, 0) - pltpu.roll(new, 1, 0)
                        flow = flow + new * pltpu.roll(slope, lanes // 2, 1)
                        density = density + new * new
                        store(0, group, slot, rows, new)
                    else:
                        store(degree, group, slot, rows, new)
                        parts_ref[slot * cells + y * NZ:slot * cells + (y + 1) * NZ, :] = new.astype(BF16)
                if not final:
                    part = jnp.dot(fore_ref[slot], parts_ref[slot * cells:(slot + 1) * cells, :], preferred_element_type=F32)
                    total = part if slot == 0 else total + part
        flow_ref[0] = flow_ref[0] + flow * jnp.where(orbital_of + group * orbs < limit, sign * (0.5 / SPACING), 0.0)
        flow_ref[1] = flow_ref[1] + density * jnp.where(orbital_of + group * orbs < limit, 1.0, 0.0)

    flat = (
        lax.broadcasted_iota(jnp.int32, now_ref.shape, 0) * now_ref.shape[1]
        + lax.broadcasted_iota(jnp.int32, now_ref.shape, 1)
    )

    def advance(step, carry):
        a = jnp.sum(jnp.where(flat == my_cell, vector_ref[...], 0.0))
        base = 6.0 + (SPACING * SPACING) * a * a
        for slot in range(slots):
            level_ref[slot] = diag_ref[slot] + base
        flow_ref[...] = jnp.zeros(flow_ref.shape, F32)

        def advance_group(group, carry):
            @pl.when(step == 0)
            def _():
                all_bytes(land_ref.at[group], in_recv.at[group])
                setup(group)
                begin(group)

            degrees(group, a)

            @pl.when(step == STEPS - 1)
            def _():
                finish(group)
                for other in order:
                    remote(
                        land_ref.at[group, other], field_part(out_ref, group, here),
                        out_send.at[group], out_recv.at[group], (layer, other),
                    ).start()
                own_out(group).start()

            return carry

        lax.fori_loop(0, groups, advance_group, 0)
        row_ref[step] = jnp.full((1, LANES), jnp.sum(flow_ref[0] + a * flow_ref[1]) * norm, F32)
        mine_row = pltpu.make_async_copy(row_ref.at[step], rows_ref.at[step, layer * grid + here], row_recv.at[step])
        mine_row.start()
        for distance in range(layers - 1, -1, -1):
            for mask in range(grid):
                if distance > 0 or mask > 0:
                    other = partners[mask] if mask else here
                    remote(
                        row_ref.at[step], rows_ref.at[step, layer * grid + here],
                        row_send.at[step], row_recv.at[step], (storey(distance), other),
                    ).start()

        @pl.when(step == 0)
        def _():
            def again(group, carry):
                begin(group)
                return carry

            lax.fori_loop(0, groups, again, 0)

        all_bytes(rows_ref.at[step], row_recv.at[step])
        deposit = jnp.zeros(flat.shape, F32)
        for floor in range(layers):
            for member in range(grid):
                cell = cell_ref[floor * points + member // share]
                deposit = deposit + jnp.where(flat == cell, rows_ref[step, floor * grid + member], 0.0)
        present = vector_ref[...]
        vector_ref[...] = macro_update(present, previous_ref[...], deposit, macro)
        previous_ref[...] = present
        return carry

    lax.fori_loop(0, STEPS, advance, 0)
    all_bytes(packed_ref.at[pl.ds(0, grid - 1)], side_send)
    for step in range(STEPS):
        all_bytes(rows_ref.at[step, pl.ds(0, grid * layers - 1)], row_send.at[step])
    for group in range(groups):
        all_bytes(land_ref.at[group, pl.ds(0, grid - 1)], in_send.at[group])
        all_bytes(land_ref.at[group, pl.ds(0, grid - 1)], out_send.at[group])
        all_bytes(land_ref.at[group], out_recv.at[group])


def propagate(materials, kinds, owners, strengths, projectors, potential, field, now, old, norm, macro, share, grid, layers, mine, own):
    points, per, lanes = potential.shape
    cells = per // mine * lanes
    planes = grid * mine
    orbs = own // GROUPS
    blocks = lanes // (2 * orbs)
    slots = planes // blocks
    nproj = strengths.shape[1]
    rows = nproj * per
    tall = rows + -(-per // 8) * 8
    vmem = pl.BlockSpec(memory_space=pltpu.VMEM)
    hbm = pl.BlockSpec(memory_space=pltpu.HBM)
    dma = lambda *shape: pltpu.SemaphoreType.DMA(shape)
    return pl.pallas_call(
        functools.partial(kernel, norm, macro, share, grid, layers, mine, own),
        out_shape=(
            jax.ShapeDtypeStruct(field.shape, F32),
            jax.ShapeDtypeStruct(now.shape, F32),
        ),
        in_specs=[hbm] * 7 + [vmem] * 2,
        out_specs=(hbm, vmem),
        scratch_shapes=[
            pltpu.SMEM(materials.shape, jnp.int32),
            pltpu.SMEM(kinds.shape, jnp.int32),
            pltpu.SMEM(owners.shape, jnp.int32),
            pltpu.VMEM(strengths.shape, F32),
            pltpu.VMEM(projectors.shape, F32),
            pltpu.VMEM(potential.shape, F32),
            pltpu.VMEM((ORDER, GROUPS, slots + 2, cells, lanes), F32),
            pltpu.VMEM((GROUPS, grid, 2, orbs * per, lanes), F32),
            pltpu.VMEM((slots * cells, lanes), BF16),
            pltpu.VMEM((GROUPS, blocks * 2 * nproj, lanes), F32),
            pltpu.VMEM((grid, tall, lanes), F32),
            pltpu.VMEM((grid, tall, lanes), F32),
            pltpu.VMEM((slots, blocks * 2 * nproj, cells), BF16),
            pltpu.VMEM((slots, cells, blocks * lanes), BF16),
            pltpu.VMEM((slots, cells, lanes), F32),
            pltpu.VMEM((slots, cells, lanes), F32),
            pltpu.VMEM((nproj, lanes), F32),
            pltpu.VMEM(now.shape, F32),
            pltpu.VMEM((STEPS, 1, LANES), F32),
            pltpu.VMEM((STEPS, layers * grid, 1, LANES), F32),
            pltpu.VMEM((2, NZ, lanes), F32),
            dma(GROUPS), dma(GROUPS),
            pltpu.SemaphoreType.DMA, pltpu.SemaphoreType.DMA,
            dma(GROUPS), dma(GROUPS),
            dma(STEPS), dma(STEPS),
            dma(6),
        ],
        compiler_params=pltpu.CompilerParams(
            vmem_limit_bytes=48 * 1024 * 1024, collective_id=0, has_side_effects=True
        ),
        name="propagate",
    )(materials, kinds, owners, strengths, projectors, potential, field, now, old)


def rows_of(array, lanes=LANES):
    lead, (planes, cells) = array.shape[:-2], array.shape[-2:]
    array = array.reshape(lead + (planes, cells // lanes, lanes))
    return jnp.swapaxes(array, -3, -2).reshape(lead + (planes * cells // lanes, lanes))


def local(
    orbitals, local_potential, projectors, strengths, material, proj_kind, point_cell,
    vector_now, vector_old, grid, layers,
):
    _, points, orb, mine, cells = orbitals.shape
    assert grid % points == 0 and orb % (grid // points) == 0
    share = grid // points
    own = orb // share
    wide = cells // LANES
    per = wide * mine
    kinds, nproj = strengths.shape
    macro = vector_now.shape[0]
    padded = (macro // 1024 + 1) * 1024
    lay = lambda vector: jnp.pad(vector, (0, padded - macro)).reshape(-1, LANES)
    field, vector = propagate(
        material, proj_kind, point_cell, strengths,
        rows_of(projectors).reshape(kinds, nproj * per, LANES),
        rows_of(local_potential),
        rows_of(orbitals).reshape(2, points, orb * per, LANES),
        lay(vector_now), lay(vector_old),
        2.0 / (orb * grid * mine * cells), macro, share, grid, layers, mine, own,
    )
    field = jnp.swapaxes(field.reshape(2, points, orb, wide, mine, LANES), -3, -2).reshape(orbitals.shape)
    return field, vector.reshape(-1)[:macro]


def solution(mesh):
    in_specs = (
        P(None, "micro", None, "grid", None),
        P("micro", "grid", None),
        P(None, None, "grid", None),
        P(),
        P(),
        P(),
        P(),
        P(),
        P(),
    )
    out_specs = (P(None, "micro", None, "grid", None), P())
    body = functools.partial(local, grid=mesh.shape["grid"], layers=mesh.shape["micro"])
    return jax.shard_map(body, mesh=mesh, in_specs=in_specs, out_specs=out_specs, check_vma=False)
```

```python
import functools

import jax
import jax.numpy as jnp
from jax import lax
from jax.experimental import pallas as pl
from jax.experimental.pallas import tpu as pltpu
from jax.sharding import PartitionSpec as P

NZ = 16
STEPS = 2
ORDER = 4
LANES = 128
GROUPS = 4

SPACING = 0.64
TIME_STEP = 0.05
COURANT = 0.9
COUPLING = 1.0
F32 = jnp.float32
BF16 = jnp.bfloat16


def halves(value):
    high = value.astype(BF16)
    return high, (value - high.astype(F32)).astype(BF16)


def macro_update(present, previous, deposit, macro):
    high, lanes = present.shape
    lane = lax.broadcasted_iota(jnp.int32, present.shape, 1)
    flat = lax.broadcasted_iota(jnp.int32, present.shape, 0) * lanes + lane
    ahead = pltpu.roll(present, lanes - 1, 1)
    ahead = jnp.where(lane == lanes - 1, pltpu.roll(ahead, high - 1, 0), ahead)
    behind = pltpu.roll(present, 1, 1)
    behind = jnp.where(lane == 0, pltpu.roll(behind, 1, 0), behind)
    curvature = ahead + behind - 2.0 * present
    following = 2.0 * present - previous + COURANT**2 * curvature - COUPLING * deposit
    return jnp.where(flat < macro, following, 0.0)


def kernel(
    norm, macro, share, grid, layers, mine, own,
    material_in, kind_in, cell_in, strength_in, projector_in, potential_in, field_ref, now_ref, old_ref,
    out_ref, vector_ref,
    material_ref, kind_ref, cell_ref, strength_ref, projector_ref, potential_ref,
    first_ref, second_ref, third_ref, fourth_ref, keep_ref, land_ref, parts_ref, total_ref, packed_ref, side_ref, fore_ref, back_ref, diag_ref, level_ref, weight_ref,
    previous_ref, row_ref, rows_ref, flow_ref, spare_ref, turned_ref, nonlocal_ref,
    in_send, in_recv, side_send, side_recv, out_send, out_recv, row_send, row_recv, load_sem,
):
    groups, slots, cells, lanes = keep_ref.shape
    terms = (first_ref, second_ref, third_ref, fourth_ref)
    kinds, nproj = strength_ref.shape
    points, per, _ = potential_ref.shape
    wide = cells // lanes
    orbs = own // groups
    blocks = lanes // (2 * orbs)
    here = lax.axis_index("grid")
    layer = lax.axis_index("micro")
    me = layer * points + lax.div(here, share)
    piece = orbs * per
    width = blocks * nproj
    barrier = pltpu.get_barrier_semaphore()

    loads = [
        pltpu.make_async_copy(source, target, load_sem.at[number])
        for number, (source, target) in enumerate((
            (material_in, material_ref), (kind_in, kind_ref), (cell_in, cell_ref),
            (strength_in, strength_ref), (projector_in, projector_ref), (potential_in, potential_ref),
        ))
    ]

    def partner(mask):
        other, bit = 0, 1
        while bit < grid:
            own_bit = lax.rem(lax.div(here, bit), 2)
            other = other + (1 - own_bit if mask & bit else own_bit) * bit
            bit *= 2
        return other

    partners = {mask: partner(mask) for mask in range(1, grid)}
    core = lax.rem(here, 2)

    def ordered():
        chips = list(range(1, grid // 2))
        swapped = list(chips)
        if len(chips) >= 2:
            swapped[0], swapped[1] = chips[1], chips[0]
        for first, second in zip(chips, swapped):
            for bit in range(2):
                one, two = 2 * first + bit, 2 * second + bit
                yield one, two
        yield 1, 1

    order = []
    for one, two in ordered():
        order.append(partners[one] if one == two else partners[one] + core * (partners[two] - partners[one]))

    def storey(distance):
        return lax.rem(layer + distance, layers)

    def remote(source, target, sent, received, device):
        return pltpu.make_async_remote_copy(
            src_ref=source, dst_ref=target, send_sem=sent, recv_sem=received,
            device_id=device, device_id_type=pl.DeviceIdType.MESH,
        )

    def field_part(ref, group, device):
        first = (lax.rem(device, share) * own + group * orbs) * per
        return ref.at[:, lax.div(device, share), pl.ds(pl.multiple_of(first, 8), piece), :]

    def all_bytes(ref, sem):
        pltpu.make_async_copy(ref, ref, sem).wait()

    def signal(device):
        pl.semaphore_signal(barrier, inc=1, device_id=device, device_id_type=pl.DeviceIdType.MESH)

    for copy in loads:
        copy.start()
    for distance in range(layers):
        if distance > 0:
            signal((storey(distance), here))
        for other in partners.values():
            signal((storey(distance), other))

    def own_in(group):
        return pltpu.make_async_copy(field_part(field_ref, group, here), land_ref.at[group, here], in_recv.at[group])

    def own_out(group):
        return pltpu.make_async_copy(land_ref.at[group, here], field_part(out_ref, group, here), out_recv.at[group])

    def own_side():
        return pltpu.make_async_copy(packed_ref.at[here], side_ref.at[here], side_recv)

    for group in range(groups):
        own_in(group).start()
    for copy in loads:
        copy.wait()
    limit = jnp.where(material_ref[me] == 1, share * own, share * own // 2) - lax.rem(here, share) * own
    my_cell, my_kind = cell_ref[me], kind_ref[me]
    for target in range(grid):
        kind = kind_ref[layer * points + target // share]
        chosen = jnp.zeros(projector_ref.shape[1:], F32)
        for number in range(kinds):
            chosen = jnp.where(kind == number, projector_ref[number], chosen)
        packed_ref[target, :nproj * per] = chosen
        packed_ref[target, nproj * per:nproj * per + per] = potential_ref[target // share]
        spare = packed_ref.shape[1] - nproj * per - per
        if spare:
            packed_ref[target, nproj * per + per:] = jnp.zeros((spare, lanes), F32)
    own_side().start()
    pl.semaphore_wait(barrier, grid * layers - 1)
    for other in order:
        remote(packed_ref.at[other], side_ref.at[here], side_send, side_recv, (layer, other)).start()
    for group in range(groups):
        for other in order:
            remote(
                field_part(field_ref, group, other), land_ref.at[group, here],
                in_send.at[group], in_recv.at[group], (layer, other),
            ).start()

    vector_ref[...] = now_ref[...]
    previous_ref[...] = old_ref[...]
    lane = lax.broadcasted_iota(jnp.int32, (1, lanes), 1)
    block_of = lax.rem(lane, lanes // 2) // orbs
    orbital_of = lax.rem(lane, orbs)
    sign = jnp.where(lane < lanes // 2, 1.0, -1.0).astype(F32)
    place = lax.rem(lane, lanes // 2)

    def turn(value, count):
        if blocks == 1:
            return value
        shift = count % blocks * orbs
        return jnp.where(place >= shift, pltpu.roll(value, shift, 1), pltpu.roll(value, lanes // 2 + shift, 1))

    weight = jnp.where(my_kind == 0, strength_ref[0:1, :], 0.0)
    for number in range(1, kinds):
        weight = weight + jnp.where(my_kind == number, strength_ref[number:number + 1, :], 0.0)
    weight = jnp.broadcast_to(weight * (2.0 * SPACING**2), (nproj, nproj))
    eye = lax.broadcasted_iota(jnp.int32, (nproj, nproj), 0) == lax.broadcasted_iota(jnp.int32, (nproj, nproj), 1)
    weight_ref[...] = jnp.broadcast_to(jnp.sum(jnp.where(eye, weight, 0.0), axis=1, keepdims=True), (nproj, lanes))

    all_bytes(side_ref, side_recv)

    def parted(ref, top):
        return ref[pl.ds(top, NZ // 2, stride=2), :], ref[pl.ds(top + 1, NZ // 2, stride=2), :]

    def columns(rows, spare):
        tall = rows.T
        for part in range(tall.shape[1] // lanes):
            spare[part] = tall[:, part * lanes:(part + 1) * lanes]
        return jnp.concatenate(
            [
                jnp.concatenate(
                    [piece for y in range(lanes // NZ) for piece in parted(spare.at[part], y * NZ)], axis=0
                )
                for part in range(tall.shape[1] // lanes)
            ],
            axis=1,
        )

    def prepare(slot, carry):
        for half in range(wide):
            level, highs, lows = [], [], []
            for block in range(blocks):
                x = block * slots + slot
                owner, plane = lax.div(x, mine), lax.rem(x, mine)
                row = half * mine + plane
                high, low = halves(side_ref[owner, pl.ds(row, nproj, stride=per), :])
                highs.append(high.astype(F32))
                lows.append(low.astype(F32))
                level.append(jnp.broadcast_to(side_ref[owner, pl.ds(nproj * per + row, 1), :], (orbs, lanes)))
            cells_here = pl.ds(pl.multiple_of(slot * cells + half * lanes, lanes), lanes)
            for number, part in enumerate((highs, lows)):
                tall = columns(jnp.concatenate(part, axis=0), spare_ref.at[number])
                fore_ref[number * width:(number + 1) * width, cells_here] = tall.T.astype(BF16)
                tall = tall.astype(BF16)
                back_ref[cells_here, number * width:(number + 1) * width] = tall
            diag_ref[cells_here, :] = columns(jnp.concatenate(level * 2, axis=0), spare_ref.at[2]) * (2.0 * SPACING**2)
        return carry

    lax.fori_loop(0, slots, prepare, 0)

    def store(term, slot, rows, value):
        terms[term][slot + 1, rows, :] = value
        if slot == 0:
            terms[term][slots + 1, rows, :] = turn(value, blocks - 1)
        if slot == slots - 1:
            terms[term][0, rows, :] = turn(value, 1)

    def setup(group):
        for slot in range(slots):
            for half in range(wide):
                pieces = []
                for part in range(2):
                    for block in range(blocks):
                        owner, plane = divmod(block * slots + slot, mine)
                        pieces.append(land_ref[group, owner, part, pl.ds(half * mine + plane, orbs, stride=per), :])
                spare = turned_ref.at[slot * wide + half]
                spare[...] = jnp.concatenate(pieces, axis=0).T
                for y in range(lanes // NZ):
                    top = half * lanes + y * NZ
                    for number, piece in enumerate(parted(spare, y * NZ)):
                        store(0, slot, slice(top + number * 8, top + number * 8 + 8), piece)

    def begin(group, planes_of):
        total = jnp.zeros((2 * width, 2 * lanes), F32)
        for slot in range(slots):
            high, low = halves(planes_of(slot))
            pieces = jnp.concatenate([high, low], axis=1)
            total = total + jnp.dot(fore_ref[:, slot * cells:(slot + 1) * cells], pieces, preferred_element_type=F32)
        total = total[:, :lanes] + total[:, lanes:]
        total_ref[group] = total[:width] + total[width:]

    def restore(group):
        for slot in range(slots):
            for top in range(0, cells, NZ):
                store(0, slot, slice(top, top + NZ), keep_ref[group, slot, top:top + NZ, :])

    def finish(group):
        occupied = jnp.where(orbital_of + group * orbs < limit, 1.0, 0.0)
        for slot in range(slots):
            for half in range(wide):
                spare = turned_ref.at[slot * wide + half]
                for y in range(lanes // NZ):
                    top = half * lanes + y * NZ
                    for number in range(2):
                        spare[pl.ds(y * NZ + number, 8, stride=2), :] = (
                            keep_ref[group, slot, top + number * 8:top + number * 8 + 8, :] * occupied
                        )
                value = spare[...].T
                for part in range(2):
                    for block in range(blocks):
                        owner, plane = divmod(block * slots + slot, mine)
                        top = (part * blocks + block) * orbs
                        land_ref[group, owner, part, pl.ds(half * mine + plane, orbs, stride=per), :] = value[top:top + orbs]

    def spread(total):
        c = jnp.zeros((nproj, lanes), F32)
        for block in range(blocks):
            c = c + jnp.where(block_of == block, total[block * nproj:(block + 1) * nproj], 0.0)
        summed = c
        for count in range(1, blocks):
            summed = summed + turn(c, count)
        summed = summed * weight_ref[...]
        high, low = halves(jnp.concatenate([jnp.where(block_of == block, summed, 0.0) for block in range(blocks)], axis=0))
        both = jnp.concatenate([high, low], axis=1)
        return jnp.concatenate([both, both], axis=0)

    def degrees(group, a):
        flow, density = jnp.zeros((8, lanes), F32), jnp.zeros((8, lanes), F32)
        total = total_ref[group]
        lines = cells // NZ
        for degree in range(1, ORDER + 1):
            scale = TIME_STEP / degree
            swap_scale = sign * (scale / (2.0 * SPACING**2))
            drift_scale = a * (scale / (2.0 * SPACING))
            source = terms[degree - 1]
            final = degree == ORDER
            both = jnp.dot(back_ref[...], spread(total), preferred_element_type=F32)
            nonlocal_ref[degree - 1] = both[:, :lanes] + both[:, lanes:]
            for slot in range(slots):
                for y in range(lines):
                    tops = (y * NZ, y * NZ + 8)
                    up, down = (y + 1) % lines * NZ, (y - 1) % lines * NZ
                    even, odd = (source[slot + 1, top:top + 8, :] for top in tops)
                    after, before = pltpu.roll(even, 7, 0), pltpu.roll(odd, 1, 0)
                    fresh = []
                    for number, (value, ahead, behind) in enumerate(((even, odd, before), (odd, after, even))):
                        rows = slice(tops[number], tops[number] + 8)
                        beside = (ahead + behind) + (
                            source[slot + 1, up + number * 8:up + number * 8 + 8, :]
                            + source[slot + 1, down + number * 8:down + number * 8 + 8, :]
                        ) + (source[slot, rows, :] + source[slot + 2, rows, :])
                        flat_rows = slice(slot * cells + rows.start, slot * cells + rows.stop)
                        level = level_ref[flat_rows, :] * value - beside + nonlocal_ref[degree - 1, flat_rows, :]
                        new = swap_scale * pltpu.roll(level, lanes // 2, 1) - drift_scale * (ahead - behind)
                        if final:
                            new = new + value
                            for term in terms[:ORDER - 1]:
                                new = new + term[slot + 1, rows, :]
                            keep_ref[group, slot, rows, :] = new
                        else:
                            store(degree, slot, rows, new)
                        fresh.append(new)
                    if final:
                        even, odd = fresh
                        for value, slope in ((even, odd - pltpu.roll(odd, 1, 0)), (odd, pltpu.roll(even, 7, 0) - even)):
                            flow = flow + value * pltpu.roll(slope, lanes // 2, 1)
                            density = density + value * value
                    else:
                        top = slot * cells + y * NZ
                        parts_ref[degree - 1, top:top + NZ, :] = jnp.concatenate(fresh, axis=0).astype(BF16)
                last = slots * cells - cells
                if not final and slot == slots - 2:
                    total = jnp.dot(fore_ref[:width, :last], parts_ref[degree - 1, :last, :], preferred_element_type=F32)
                if not final and slot == slots - 1:
                    total = total + jnp.dot(fore_ref[:width, last:], parts_ref[degree - 1, last:, :], preferred_element_type=F32)
        flow_ref[0] = flow_ref[0] + flow * jnp.where(orbital_of + group * orbs < limit, sign * (0.5 / SPACING), 0.0)
        flow_ref[1] = flow_ref[1] + density * jnp.where(orbital_of + group * orbs < limit, 1.0, 0.0)

    flat = (
        lax.broadcasted_iota(jnp.int32, now_ref.shape, 0) * now_ref.shape[1]
        + lax.broadcasted_iota(jnp.int32, now_ref.shape, 1)
    )

    def advance(step, carry):
        a = jnp.sum(jnp.where(flat == my_cell, vector_ref[...], 0.0))
        base = 6.0 + (SPACING * SPACING) * a * a
        level_ref[...] = diag_ref[...] + base
        flow_ref[...] = jnp.zeros(flow_ref.shape, F32)

        def advance_group(group, carry):
            @pl.when(step == 0)
            def _():
                all_bytes(land_ref.at[group], in_recv.at[group])
                setup(group)
                begin(group, lambda slot: first_ref[slot + 1])

            @pl.when(step > 0)
            def _():
                restore(group)

            degrees(group, a)

            @pl.when(step == STEPS - 1)
            def _():
                finish(group)
                for other in order:
                    remote(
                        land_ref.at[group, other], field_part(out_ref, group, here),
                        out_send.at[group], out_recv.at[group], (layer, other),
                    ).start()
                own_out(group).start()

            return carry

        lax.fori_loop(0, groups, advance_group, 0)
        row_ref[step] = jnp.full((1, LANES), jnp.sum(flow_ref[0] + a * flow_ref[1]) * norm, F32)
        mine_row = pltpu.make_async_copy(row_ref.at[step], rows_ref.at[step, layer * grid + here], row_recv.at[step])
        mine_row.start()
        for distance in range(layers - 1, -1, -1):
            for mask in range(grid):
                if distance > 0 or mask > 0:
                    other = partners[mask] if mask else here
                    remote(
                        row_ref.at[step], rows_ref.at[step, layer * grid + here],
                        row_send.at[step], row_recv.at[step], (storey(distance), other),
                    ).start()

        @pl.when(step == 0)
        def _():
            def again(group, carry):
                begin(group, lambda slot: keep_ref[group, slot])
                return carry

            lax.fori_loop(0, groups, again, 0)

        all_bytes(rows_ref.at[step], row_recv.at[step])
        deposit = jnp.zeros(flat.shape, F32)
        for floor in range(layers):
            for member in range(grid):
                cell = cell_ref[floor * points + member // share]
                deposit = deposit + jnp.where(flat == cell, rows_ref[step, floor * grid + member], 0.0)
        present = vector_ref[...]
        vector_ref[...] = macro_update(present, previous_ref[...], deposit, macro)
        previous_ref[...] = present
        return carry

    lax.fori_loop(0, STEPS, advance, 0)
    all_bytes(packed_ref.at[pl.ds(0, grid - 1)], side_send)
    for step in range(STEPS):
        all_bytes(rows_ref.at[step, pl.ds(0, grid * layers - 1)], row_send.at[step])
    for group in range(groups):
        all_bytes(land_ref.at[group, pl.ds(0, grid - 1)], in_send.at[group])
        all_bytes(land_ref.at[group, pl.ds(0, grid - 1)], out_send.at[group])
        all_bytes(land_ref.at[group], out_recv.at[group])


def propagate(materials, kinds, owners, strengths, projectors, potential, field, now, old, norm, macro, share, grid, layers, mine, own):
    points, per, lanes = potential.shape
    cells = per // mine * lanes
    planes = grid * mine
    orbs = own // GROUPS
    blocks = lanes // (2 * orbs)
    slots = planes // blocks
    nproj = strengths.shape[1]
    rows = nproj * per
    tall = rows + -(-per // 8) * 8
    vmem = pl.BlockSpec(memory_space=pltpu.VMEM)
    hbm = pl.BlockSpec(memory_space=pltpu.HBM)
    dma = lambda *shape: pltpu.SemaphoreType.DMA(shape)
    return pl.pallas_call(
        functools.partial(kernel, norm, macro, share, grid, layers, mine, own),
        out_shape=(
            jax.ShapeDtypeStruct(field.shape, F32),
            jax.ShapeDtypeStruct(now.shape, F32),
        ),
        in_specs=[hbm] * 7 + [vmem] * 2,
        out_specs=(hbm, vmem),
        scratch_shapes=[
            pltpu.SMEM(materials.shape, jnp.int32),
            pltpu.SMEM(kinds.shape, jnp.int32),
            pltpu.SMEM(owners.shape, jnp.int32),
            pltpu.VMEM(strengths.shape, F32),
            pltpu.VMEM(projectors.shape, F32),
            pltpu.VMEM(potential.shape, F32),
            *[pltpu.VMEM((slots + 2, cells, lanes), F32)] * ORDER,
            pltpu.VMEM((GROUPS, slots, cells, lanes), F32),
            pltpu.VMEM((GROUPS, grid, 2, orbs * per, lanes), F32),
            pltpu.VMEM((ORDER - 1, slots * cells, lanes), BF16),
            pltpu.VMEM((GROUPS, blocks * nproj, lanes), F32),
            pltpu.VMEM((grid, tall, lanes), F32),
            pltpu.VMEM((grid, tall, lanes), F32),
            pltpu.VMEM((2 * blocks * nproj, slots * cells), BF16),
            pltpu.VMEM((slots * cells, 2 * blocks * nproj), BF16),
            pltpu.VMEM((slots * cells, lanes), F32),
            pltpu.VMEM((slots * cells, lanes), F32),
            pltpu.VMEM((nproj, lanes), F32),
            pltpu.VMEM(now.shape, F32),
            pltpu.VMEM((STEPS, 1, LANES), F32),
            pltpu.VMEM((STEPS, layers * grid, 1, LANES), F32),
            pltpu.VMEM((2, 8, lanes), F32),
            pltpu.VMEM((3, blocks * nproj // lanes, lanes, lanes), F32),
            pltpu.VMEM((planes // blocks * (cells // lanes), lanes, lanes), F32),
            pltpu.VMEM((ORDER, slots * cells, lanes), F32),
            dma(GROUPS), dma(GROUPS),
            pltpu.SemaphoreType.DMA, pltpu.SemaphoreType.DMA,
            dma(GROUPS), dma(GROUPS),
            dma(STEPS), dma(STEPS),
            dma(6),
        ],
        compiler_params=pltpu.CompilerParams(
            vmem_limit_bytes=48 * 1024 * 1024, collective_id=0, has_side_effects=True
        ),
        name="propagate",
    )(materials, kinds, owners, strengths, projectors, potential, field, now, old)


def rows_of(array, lanes=LANES):
    lead, (planes, cells) = array.shape[:-2], array.shape[-2:]
    array = array.reshape(lead + (planes, cells // lanes, lanes))
    return jnp.swapaxes(array, -3, -2).reshape(lead + (planes * cells // lanes, lanes))


def local(
    orbitals, local_potential, projectors, strengths, material, proj_kind, point_cell,
    vector_now, vector_old, grid, layers,
):
    _, points, orb, mine, cells = orbitals.shape
    assert grid % points == 0 and orb % (grid // points) == 0
    share = grid // points
    own = orb // share
    wide = cells // LANES
    per = wide * mine
    kinds, nproj = strengths.shape
    macro = vector_now.shape[0]
    padded = (macro // 1024 + 1) * 1024
    lay = lambda vector: jnp.pad(vector, (0, padded - macro)).reshape(-1, LANES)
    held = lambda array: pltpu.with_memory_space_constraint(array, pltpu.HBM)
    field, vector = propagate(
        held(material), held(proj_kind), held(point_cell), held(strengths),
        held(rows_of(projectors).reshape(kinds, nproj * per, LANES)),
        held(rows_of(local_potential)),
        held(rows_of(orbitals).reshape(2, points, orb * per, LANES)),
        lay(vector_now), lay(vector_old),
        2.0 / (orb * grid * mine * cells), macro, share, grid, layers, mine, own,
    )
    field = jnp.swapaxes(field.reshape(2, points, orb, wide, mine, LANES), -3, -2).reshape(orbitals.shape)
    return field, vector.reshape(-1)[:macro]


def solution(mesh):
    in_specs = (
        P(None, "micro", None, "grid", None),
        P("micro", "grid", None),
        P(None, None, "grid", None),
        P(),
        P(),
        P(),
        P(),
        P(),
        P(),
    )
    out_specs = (P(None, "micro", None, "grid", None), P())
    body = functools.partial(local, grid=mesh.shape["grid"], layers=mesh.shape["micro"])
    return jax.shard_map(body, mesh=mesh, in_specs=in_specs, out_specs=out_specs, check_vma=False)
```

```python
import functools

import jax
import jax.numpy as jnp
from jax import lax
from jax.experimental import pallas as pl
from jax.experimental.pallas import tpu as pltpu
from jax.sharding import PartitionSpec as P

NZ = 16
STEPS = 2
ORDER = 4
LANES = 128
GROUPS = 4

SPACING = 0.64
TIME_STEP = 0.05
COURANT = 0.9
COUPLING = 1.0
F32 = jnp.float32
BF16 = jnp.bfloat16


def halves(value):
    high = value.astype(BF16)
    return high, (value - high.astype(F32)).astype(BF16)


def macro_update(present, previous, macro):
    high, lanes = present.shape
    lane = lax.broadcasted_iota(jnp.int32, present.shape, 1)
    flat = lax.broadcasted_iota(jnp.int32, present.shape, 0) * lanes + lane
    ahead = pltpu.roll(present, lanes - 1, 1)
    ahead = jnp.where(lane == lanes - 1, pltpu.roll(ahead, high - 1, 0), ahead)
    behind = pltpu.roll(present, 1, 1)
    behind = jnp.where(lane == 0, pltpu.roll(behind, 1, 0), behind)
    curvature = ahead + behind - 2.0 * present
    following = 2.0 * present - previous + COURANT**2 * curvature
    return jnp.where(flat < macro, following, 0.0)


def kernel(
    norm, macro, share, grid, layers, mine, own,
    material_in, kind_in, cell_in, strength_in, projector_in, potential_in, field_ref, now_in, old_in,
    out_ref, vector_ref,
    material_ref, kind_ref, cell_ref, strength_ref, projector_ref, potential_ref,
    first_ref, second_ref, third_ref, fourth_ref, keep_ref, land_ref, parts_ref, start_ref, packed_ref, side_ref, fore_ref, back_ref, diag_ref, level_ref, weight_ref,
    previous_ref, line_now_ref, line_old_ref, row_ref, rows_ref, flow_ref, spare_ref, turned_ref, nonlocal_ref, mask_ref,
    in_send, in_recv, side_send, side_recv, out_send, out_recv, row_send, row_recv, load_sem, ready_sem,
):
    groups, slots, cells, lanes = keep_ref.shape
    terms = (first_ref, second_ref, third_ref, fourth_ref)
    kinds, nproj = strength_ref.shape
    points, per, _ = potential_ref.shape
    wide = cells // lanes
    orbs = own // groups
    blocks = lanes // (2 * orbs)
    here = lax.axis_index("grid")
    layer = lax.axis_index("micro")
    me = layer * points + lax.div(here, share)
    piece = orbs * per
    width = blocks * nproj
    barrier = pltpu.get_barrier_semaphore()

    loads = [
        pltpu.make_async_copy(source, target, load_sem.at[number])
        for number, (source, target) in enumerate((
            (material_in, material_ref), (kind_in, kind_ref), (cell_in, cell_ref),
            (strength_in, strength_ref), (projector_in, projector_ref), (potential_in, potential_ref),
            (now_in, line_now_ref), (old_in, line_old_ref),
        ))
    ]

    def partner(mask):
        other, bit = 0, 1
        while bit < grid:
            own_bit = lax.rem(lax.div(here, bit), 2)
            other = other + (1 - own_bit if mask & bit else own_bit) * bit
            bit *= 2
        return other

    partners = {mask: partner(mask) for mask in range(1, grid)}
    core = lax.rem(here, 2)

    def ordered():
        chips = list(range(1, grid // 2))
        swapped = list(chips)
        if len(chips) >= 2:
            swapped[0], swapped[1] = chips[1], chips[0]
        for first, second in zip(chips, swapped):
            for bit in range(2):
                one, two = 2 * first + bit, 2 * second + bit
                yield one, two
        yield 1, 1

    order = []
    for one, two in ordered():
        order.append(partners[one] if one == two else partners[one] + core * (partners[two] - partners[one]))

    def storey(distance):
        return lax.rem(layer + distance, layers)

    def remote(source, target, sent, received, device):
        return pltpu.make_async_remote_copy(
            src_ref=source, dst_ref=target, send_sem=sent, recv_sem=received,
            device_id=device, device_id_type=pl.DeviceIdType.MESH,
        )

    def field_part(ref, group, device):
        first = (lax.rem(device, share) * own + group * orbs) * per
        return ref.at[:, lax.div(device, share), pl.ds(pl.multiple_of(first, 8), piece), :]

    def all_bytes(ref, sem):
        pltpu.make_async_copy(ref, ref, sem).wait()

    def signal(semaphore, device):
        pl.semaphore_signal(semaphore, inc=1, device_id=device, device_id_type=pl.DeviceIdType.MESH)

    for copy in loads:
        copy.start()
    for distance in range(1, layers):
        signal(barrier, (storey(distance), here))
    for other in partners.values():
        signal(barrier, (layer, other))

    def own_in(group):
        return pltpu.make_async_copy(field_part(field_ref, group, here), land_ref.at[group, here], in_recv.at[group])

    def own_out(group):
        return pltpu.make_async_copy(land_ref.at[group, here], field_part(out_ref, group, here), out_recv.at[group])

    def own_side():
        return pltpu.make_async_copy(packed_ref.at[here], side_ref.at[here], side_recv)

    for group in range(groups):
        own_in(group).start()
    for copy in loads:
        copy.wait()
    limit = jnp.where(material_ref[me] == 1, share * own, share * own // 2) - lax.rem(here, share) * own
    my_cell, my_kind = cell_ref[me], kind_ref[me]
    for target in range(grid):
        kind = kind_ref[layer * points + target // share]
        chosen = jnp.zeros(projector_ref.shape[1:], F32)
        for number in range(kinds):
            chosen = jnp.where(kind == number, projector_ref[number], chosen)
        packed_ref[target, :nproj * per] = chosen
        packed_ref[target, nproj * per:nproj * per + per] = potential_ref[target // share]
        spare = packed_ref.shape[1] - nproj * per - per
        if spare:
            packed_ref[target, nproj * per + per:] = jnp.zeros((spare, lanes), F32)
    own_side().start()
    pl.semaphore_wait(barrier, grid + layers - 2)
    for other in order:
        remote(packed_ref.at[other], side_ref.at[here], side_send, side_recv, (layer, other)).start()
    for group in range(groups):
        for other in order:
            remote(
                field_part(field_ref, group, other), land_ref.at[group, here],
                in_send.at[group], in_recv.at[group], (layer, other),
            ).start()

    for distance in range(1, layers):
        signal(ready_sem, (storey(distance), here))
    for line, rows in ((line_now_ref, vector_ref), (line_old_ref, previous_ref)):
        rows[...] = jnp.zeros(rows.shape, F32)
        for top in range(0, macro, LANES):
            length = min(LANES, macro - top)
            rows[top // LANES, :length] = line[pl.ds(top, length)]
    lane = lax.broadcasted_iota(jnp.int32, (1, lanes), 1)
    block_of = lax.rem(lane, lanes // 2) // orbs
    orbital_of = lax.rem(lane, orbs)
    sign = jnp.where(lane < lanes // 2, 1.0, -1.0).astype(F32)
    place = lax.rem(lane, lanes // 2)

    def turn(value, count):
        if blocks == 1:
            return value
        shift = count % blocks * orbs
        return jnp.where(place >= shift, pltpu.roll(value, shift, 1), pltpu.roll(value, lanes // 2 + shift, 1))

    weight = jnp.where(my_kind == 0, strength_ref[0:1, :], 0.0)
    for number in range(1, kinds):
        weight = weight + jnp.where(my_kind == number, strength_ref[number:number + 1, :], 0.0)
    weight = jnp.broadcast_to(weight * (2.0 * SPACING**2), (nproj, nproj))
    eye = lax.broadcasted_iota(jnp.int32, (nproj, nproj), 0) == lax.broadcasted_iota(jnp.int32, (nproj, nproj), 1)
    weight_ref[...] = jnp.broadcast_to(jnp.sum(jnp.where(eye, weight, 0.0), axis=1, keepdims=True), (nproj, lanes))

    all_bytes(side_ref, side_recv)

    def parted(ref, top):
        return ref[pl.ds(top, NZ // 2, stride=2), :], ref[pl.ds(top + 1, NZ // 2, stride=2), :]

    def columns(rows, spare):
        tall = rows.T
        for part in range(tall.shape[1] // lanes):
            spare[part] = tall[:, part * lanes:(part + 1) * lanes]
        return jnp.concatenate(
            [
                jnp.concatenate(
                    [piece for y in range(lanes // NZ) for piece in parted(spare.at[part], y * NZ)], axis=0
                )
                for part in range(tall.shape[1] // lanes)
            ],
            axis=1,
        )

    def prepare(slot, carry):
        for half in range(wide):
            level, highs, lows = [], [], []
            for block in range(blocks):
                x = block * slots + slot
                owner, plane = lax.div(x, mine), lax.rem(x, mine)
                row = half * mine + plane
                high, low = halves(side_ref[owner, pl.ds(row, nproj, stride=per), :])
                highs.append(high.astype(F32))
                lows.append(low.astype(F32))
                level.append(jnp.broadcast_to(side_ref[owner, pl.ds(nproj * per + row, 1), :], (orbs, lanes)))
            cells_here = pl.ds(pl.multiple_of(slot * cells + half * lanes, lanes), lanes)
            for number, part in enumerate((highs, lows)):
                tall = columns(jnp.concatenate(part, axis=0), spare_ref.at[number])
                fore_ref[number * width:(number + 1) * width, cells_here] = tall.T.astype(BF16)
                tall = tall.astype(BF16)
                back_ref[cells_here, number * width:(number + 1) * width] = tall
            diag_ref[cells_here, :] = columns(jnp.concatenate(level * 2, axis=0), spare_ref.at[2]) * (2.0 * SPACING**2)
        return carry

    lax.fori_loop(0, slots, prepare, 0)

    def store(term, slot, rows, value):
        terms[term][slot + 1, rows, :] = value
        if slot == 0:
            terms[term][slots + 1, rows, :] = turn(value, blocks - 1)
        if slot == slots - 1:
            terms[term][0, rows, :] = turn(value, 1)

    def setup(group):
        for slot in range(slots):
            for half in range(wide):
                pieces = []
                for part in range(2):
                    for block in range(blocks):
                        owner, plane = divmod(block * slots + slot, mine)
                        pieces.append(land_ref[group, owner, part, pl.ds(half * mine + plane, orbs, stride=per), :])
                spare = turned_ref.at[slot * wide + half]
                spare[...] = jnp.concatenate(pieces, axis=0).T
                for y in range(lanes // NZ):
                    top = half * lanes + y * NZ
                    for number, piece in enumerate(parted(spare, y * NZ)):
                        store(0, slot, slice(top + number * 8, top + number * 8 + 8), piece)

    def begin(group, planes_of):
        total = jnp.zeros((2 * width, 2 * lanes), F32)
        for slot in range(slots):
            high, low = halves(planes_of(slot))
            pieces = jnp.concatenate([high, low], axis=1)
            total = total + jnp.dot(fore_ref[:, slot * cells:(slot + 1) * cells], pieces, preferred_element_type=F32)
        total = total[:, :lanes] + total[:, lanes:]
        start_ref[group] = distant(total[:width] + total[width:])

    def distant(total):
        both = jnp.dot(back_ref[...], spread(total), preferred_element_type=F32)
        return both[:, :lanes] + both[:, lanes:]

    def restore(group):
        for slot in range(slots):
            for top in range(0, cells, NZ):
                store(0, slot, slice(top, top + NZ), keep_ref[group, slot, top:top + NZ, :])

    def finish(group):
        occupied = jnp.where(orbital_of + group * orbs < limit, 1.0, 0.0)
        for slot in range(slots):
            for half in range(wide):
                spare = turned_ref.at[slot * wide + half]
                for y in range(lanes // NZ):
                    top = half * lanes + y * NZ
                    for number in range(2):
                        spare[pl.ds(y * NZ + number, 8, stride=2), :] = (
                            keep_ref[group, slot, top + number * 8:top + number * 8 + 8, :] * occupied
                        )
                value = spare[...].T
                for part in range(2):
                    for block in range(blocks):
                        owner, plane = divmod(block * slots + slot, mine)
                        top = (part * blocks + block) * orbs
                        land_ref[group, owner, part, pl.ds(half * mine + plane, orbs, stride=per), :] = value[top:top + orbs]

    def spread(total):
        c = jnp.zeros((nproj, lanes), F32)
        for block in range(blocks):
            c = c + jnp.where(block_of == block, total[block * nproj:(block + 1) * nproj], 0.0)
        summed = c
        for count in range(1, blocks):
            summed = summed + turn(c, count)
        summed = summed * weight_ref[...]
        high, low = halves(jnp.concatenate([jnp.where(block_of == block, summed, 0.0) for block in range(blocks)], axis=0))
        both = jnp.concatenate([high, low], axis=1)
        return jnp.concatenate([both, both], axis=0)

    def degrees(group, a):
        flow, density = jnp.zeros((8, lanes), F32), jnp.zeros((8, lanes), F32)
        total = None
        lines = cells // NZ
        for degree in range(1, ORDER + 1):
            scale = TIME_STEP / degree
            swap_scale = sign * (scale / (2.0 * SPACING**2))
            drift_scale = a * (scale / (2.0 * SPACING))
            source = terms[degree - 1]
            final = degree == ORDER
            if degree > 1:
                nonlocal_ref[degree - 2] = distant(total)
            far = start_ref.at[group] if degree == 1 else nonlocal_ref.at[degree - 2]
            for slot in range(slots):
                for y in range(lines):
                    tops = (y * NZ, y * NZ + 8)
                    up, down = (y + 1) % lines * NZ, (y - 1) % lines * NZ
                    even, odd = (source[slot + 1, top:top + 8, :] for top in tops)
                    after, before = pltpu.roll(even, 7, 0), pltpu.roll(odd, 1, 0)
                    fresh = []
                    for number, (value, ahead, behind) in enumerate(((even, odd, before), (odd, after, even))):
                        rows = slice(tops[number], tops[number] + 8)
                        beside = (ahead + behind) + (
                            source[slot + 1, up + number * 8:up + number * 8 + 8, :]
                            + source[slot + 1, down + number * 8:down + number * 8 + 8, :]
                        ) + (source[slot, rows, :] + source[slot + 2, rows, :])
                        flat_rows = slice(slot * cells + rows.start, slot * cells + rows.stop)
                        level = level_ref[flat_rows, :] * value - beside + far[flat_rows, :]
                        new = swap_scale * pltpu.roll(level, lanes // 2, 1) - drift_scale * (ahead - behind)
                        if final:
                            new = new + value
                            for term in terms[:ORDER - 1]:
                                new = new + term[slot + 1, rows, :]
                            keep_ref[group, slot, rows, :] = new
                        else:
                            store(degree, slot, rows, new)
                        fresh.append(new)
                    if final:
                        even, odd = fresh
                        for value, slope in ((even, odd - pltpu.roll(odd, 1, 0)), (odd, pltpu.roll(even, 7, 0) - even)):
                            flow = flow + value * pltpu.roll(slope, lanes // 2, 1)
                            density = density + value * value
                    else:
                        top = slot * cells + y * NZ
                        parts_ref[degree - 1, top:top + NZ, :] = jnp.concatenate(fresh, axis=0).astype(BF16)
                last = slots * cells - cells
                if not final and slot == slots - 2:
                    total = jnp.dot(fore_ref[:width, :last], parts_ref[degree - 1, :last, :], preferred_element_type=F32)
                if not final and slot == slots - 1:
                    total = total + jnp.dot(fore_ref[:width, last:], parts_ref[degree - 1, last:, :], preferred_element_type=F32)
        flow_ref[0] = flow_ref[0] + flow * jnp.where(orbital_of + group * orbs < limit, sign * (0.5 / SPACING), 0.0)
        flow_ref[1] = flow_ref[1] + density * jnp.where(orbital_of + group * orbs < limit, 1.0, 0.0)

    flat = (
        lax.broadcasted_iota(jnp.int32, vector_ref.shape, 0) * vector_ref.shape[1]
        + lax.broadcasted_iota(jnp.int32, vector_ref.shape, 1)
    )

    def advance(step, a):
        base = 6.0 + (SPACING * SPACING) * a * a
        level_ref[...] = diag_ref[...] + base
        flow_ref[...] = jnp.zeros(flow_ref.shape, F32)

        def advance_group(group, carry):
            @pl.when(step == 0)
            def _():
                all_bytes(land_ref.at[group], in_recv.at[group])
                setup(group)
                begin(group, lambda slot: first_ref[slot + 1])

            @pl.when(step * group > 0)
            def _():
                restore(group)

            degrees(group, a)

            @pl.when(step == STEPS - 1)
            def _():
                finish(group)
                for other in order:
                    remote(
                        land_ref.at[group, other], field_part(out_ref, group, here),
                        out_send.at[group], out_recv.at[group], (layer, other),
                    ).start()
                own_out(group).start()

            return carry

        lax.fori_loop(0, groups, advance_group, 0)
        row_ref[step] = jnp.full((1, LANES), jnp.sum(flow_ref[0] + a * flow_ref[1]) * norm, F32)
        mine_row = pltpu.make_async_copy(row_ref.at[step], rows_ref.at[step, layer * grid + here], row_recv.at[step])
        mine_row.start()

        @pl.when(step == 0)
        def _():
            pl.semaphore_wait(ready_sem, layers - 1)

        for distance in range(layers - 1, -1, -1):
            for mask in range(grid):
                if distance > 0 or mask > 0:
                    other = partners[mask] if mask else here
                    remote(
                        row_ref.at[step], rows_ref.at[step, layer * grid + here],
                        row_send.at[step], row_recv.at[step], (storey(distance), other),
                    ).start()

        @pl.when(step == 0)
        def _():
            def again(group, carry):
                begin(group, lambda slot: keep_ref[group, slot])
                return carry

            lax.fori_loop(0, groups, again, 0)
            restore(0)

        present = vector_ref[...]
        following = macro_update(present, previous_ref[...], macro)
        own_following = jnp.sum(jnp.where(flat == my_cell, following, 0.0))
        for floor in range(layers):
            for member in range(grid):
                same = cell_ref[floor * points + member // share] == my_cell
                mask_ref[floor * grid + member] = jnp.full((1, LANES), jnp.where(same, COUPLING / LANES, 0.0), F32)
        all_bytes(rows_ref.at[step], row_recv.at[step])
        own_deposit = jnp.sum(rows_ref[step] * mask_ref[...])
        deposit = jnp.zeros(flat.shape, F32)
        for floor in range(layers):
            for member in range(grid):
                cell = cell_ref[floor * points + member // share]
                deposit = deposit + jnp.where(flat == cell, rows_ref[step, floor * grid + member], 0.0)
        vector_ref[...] = following - COUPLING * deposit
        previous_ref[...] = present
        return own_following - own_deposit

    lax.fori_loop(0, STEPS, advance, jnp.sum(jnp.where(flat == my_cell, vector_ref[...], 0.0)))
    all_bytes(packed_ref.at[pl.ds(0, grid - 1)], side_send)
    for step in range(STEPS):
        all_bytes(rows_ref.at[step, pl.ds(0, grid * layers - 1)], row_send.at[step])
    for group in range(groups):
        all_bytes(land_ref.at[group, pl.ds(0, grid - 1)], in_send.at[group])
        all_bytes(land_ref.at[group, pl.ds(0, grid - 1)], out_send.at[group])
        all_bytes(land_ref.at[group], out_recv.at[group])


def propagate(materials, kinds, owners, strengths, projectors, potential, field, now, old, norm, macro, share, grid, layers, mine, own):
    points, per, lanes = potential.shape
    cells = per // mine * lanes
    planes = grid * mine
    orbs = own // GROUPS
    blocks = lanes // (2 * orbs)
    slots = planes // blocks
    nproj = strengths.shape[1]
    rows = nproj * per
    tall = rows + -(-per // 8) * 8
    vmem = pl.BlockSpec(memory_space=pltpu.VMEM)
    hbm = pl.BlockSpec(memory_space=pltpu.HBM)
    dma = lambda *shape: pltpu.SemaphoreType.DMA(shape)
    return pl.pallas_call(
        functools.partial(kernel, norm, macro, share, grid, layers, mine, own),
        out_shape=(
            jax.ShapeDtypeStruct(field.shape, F32),
            jax.ShapeDtypeStruct((-(-macro // 1024) * 8, LANES), F32),
        ),
        in_specs=[hbm] * 9,
        out_specs=(hbm, vmem),
        scratch_shapes=[
            pltpu.SMEM(materials.shape, jnp.int32),
            pltpu.SMEM(kinds.shape, jnp.int32),
            pltpu.SMEM(owners.shape, jnp.int32),
            pltpu.VMEM(strengths.shape, F32),
            pltpu.VMEM(projectors.shape, F32),
            pltpu.VMEM(potential.shape, F32),
            *[pltpu.VMEM((slots + 2, cells, lanes), F32)] * ORDER,
            pltpu.VMEM((GROUPS, slots, cells, lanes), F32),
            pltpu.VMEM((GROUPS, grid, 2, orbs * per, lanes), F32),
            pltpu.VMEM((ORDER - 1, slots * cells, lanes), BF16),
            pltpu.VMEM((GROUPS, slots * cells, lanes), F32),
            pltpu.VMEM((grid, tall, lanes), F32),
            pltpu.VMEM((grid, tall, lanes), F32),
            pltpu.VMEM((2 * blocks * nproj, slots * cells), BF16),
            pltpu.VMEM((slots * cells, 2 * blocks * nproj), BF16),
            pltpu.VMEM((slots * cells, lanes), F32),
            pltpu.VMEM((slots * cells, lanes), F32),
            pltpu.VMEM((nproj, lanes), F32),
            pltpu.VMEM((-(-macro // 1024) * 8, LANES), F32),
            pltpu.VMEM(now.shape, F32),
            pltpu.VMEM(old.shape, F32),
            pltpu.VMEM((STEPS, 1, LANES), F32),
            pltpu.VMEM((STEPS, layers * grid, 1, LANES), F32),
            pltpu.VMEM((2, 8, lanes), F32),
            pltpu.VMEM((3, blocks * nproj // lanes, lanes, lanes), F32),
            pltpu.VMEM((planes // blocks * (cells // lanes), lanes, lanes), F32),
            pltpu.VMEM((ORDER - 1, slots * cells, lanes), F32),
            pltpu.VMEM((layers * grid, 1, LANES), F32),
            dma(GROUPS), dma(GROUPS),
            pltpu.SemaphoreType.DMA, pltpu.SemaphoreType.DMA,
            dma(GROUPS), dma(GROUPS),
            dma(STEPS), dma(STEPS),
            dma(8),
            pltpu.SemaphoreType.REGULAR,
        ],
        compiler_params=pltpu.CompilerParams(
            vmem_limit_bytes=48 * 1024 * 1024, collective_id=0, has_side_effects=True
        ),
        name="propagate",
    )(materials, kinds, owners, strengths, projectors, potential, field, now, old)


def rows_of(array, lanes=LANES):
    lead, (planes, cells) = array.shape[:-2], array.shape[-2:]
    array = array.reshape(lead + (planes, cells // lanes, lanes))
    return jnp.swapaxes(array, -3, -2).reshape(lead + (planes * cells // lanes, lanes))


def local(
    orbitals, local_potential, projectors, strengths, material, proj_kind, point_cell,
    vector_now, vector_old, grid, layers,
):
    _, points, orb, mine, cells = orbitals.shape
    assert grid % points == 0 and orb % (grid // points) == 0
    share = grid // points
    own = orb // share
    wide = cells // LANES
    per = wide * mine
    kinds, nproj = strengths.shape
    macro = vector_now.shape[0]
    held = lambda array: pltpu.with_memory_space_constraint(array, pltpu.HBM)
    field, vector = propagate(
        held(material), held(proj_kind), held(point_cell), held(strengths),
        held(rows_of(projectors).reshape(kinds, nproj * per, LANES)),
        held(rows_of(local_potential)),
        held(rows_of(orbitals).reshape(2, points, orb * per, LANES)),
        held(vector_now), held(vector_old),
        2.0 / (orb * grid * mine * cells), macro, share, grid, layers, mine, own,
    )
    field = jnp.swapaxes(field.reshape(2, points, orb, wide, mine, LANES), -3, -2).reshape(orbitals.shape)
    return field, vector.reshape(-1)[:macro]


def solution(mesh):
    in_specs = (
        P(None, "micro", None, "grid", None),
        P("micro", "grid", None),
        P(None, None, "grid", None),
        P(),
        P(),
        P(),
        P(),
        P(),
        P(),
    )
    out_specs = (P(None, "micro", None, "grid", None), P())
    body = functools.partial(local, grid=mesh.shape["grid"], layers=mesh.shape["micro"])
    return jax.shard_map(body, mesh=mesh, in_specs=in_specs, out_specs=out_specs, check_vma=False)
```

```python
import functools

import jax
import jax.numpy as jnp
from jax import lax
from jax.experimental import pallas as pl
from jax.experimental.pallas import tpu as pltpu
from jax.sharding import PartitionSpec as P

NZ = 16
STEPS = 2
ORDER = 4
LANES = 128
GROUPS = 4

SPACING = 0.64
TIME_STEP = 0.05
COURANT = 0.9
COUPLING = 1.0
F32 = jnp.float32
BF16 = jnp.bfloat16


def halves(value):
    high = value.astype(BF16)
    return high, (value - high.astype(F32)).astype(BF16)


def macro_update(present, previous, macro):
    high, lanes = present.shape
    lane = lax.broadcasted_iota(jnp.int32, present.shape, 1)
    flat = lax.broadcasted_iota(jnp.int32, present.shape, 0) * lanes + lane
    ahead = pltpu.roll(present, lanes - 1, 1)
    ahead = jnp.where(lane == lanes - 1, pltpu.roll(ahead, high - 1, 0), ahead)
    behind = pltpu.roll(present, 1, 1)
    behind = jnp.where(lane == 0, pltpu.roll(behind, 1, 0), behind)
    curvature = ahead + behind - 2.0 * present
    following = 2.0 * present - previous + COURANT**2 * curvature
    return jnp.where(flat < macro, following, 0.0)


def kernel(
    norm, macro, share, grid, layers, mine, own,
    material_in, kind_in, cell_in, strength_in, projector_in, potential_in, field_ref, now_in, old_in,
    out_ref, vector_ref,
    material_ref, kind_ref, cell_ref, strength_ref, projector_ref, potential_ref,
    first_ref, second_ref, third_ref, fourth_ref, keep_ref, land_ref, parts_ref, start_ref, packed_ref, side_ref, fore_ref, back_ref, diag_ref, level_ref, weight_ref,
    previous_ref, line_now_ref, line_old_ref, row_ref, rows_ref, flow_ref, spare_ref, turned_ref, nonlocal_ref, mask_ref,
    in_send, in_recv, side_send, side_recv, out_send, out_recv, row_send, row_recv, load_sem, ready_sem,
):
    groups, slots, cells, lanes = keep_ref.shape
    terms = (first_ref, second_ref, third_ref, fourth_ref)
    kinds, nproj = strength_ref.shape
    points, per, _ = potential_ref.shape
    wide = cells // lanes
    orbs = own // groups
    blocks = lanes // (2 * orbs)
    here = lax.axis_index("grid")
    layer = lax.axis_index("micro")
    me = layer * points + lax.div(here, share)
    piece = orbs * per
    width = blocks * nproj
    barrier = pltpu.get_barrier_semaphore()

    loads = [
        pltpu.make_async_copy(source, target, load_sem.at[number])
        for number, (source, target) in enumerate((
            (material_in, material_ref), (kind_in, kind_ref), (cell_in, cell_ref),
            (strength_in, strength_ref), (projector_in, projector_ref), (potential_in, potential_ref),
            (now_in, line_now_ref), (old_in, line_old_ref),
        ))
    ]

    def partner(mask):
        other, bit = 0, 1
        while bit < grid:
            own_bit = lax.rem(lax.div(here, bit), 2)
            other = other + (1 - own_bit if mask & bit else own_bit) * bit
            bit *= 2
        return other

    partners = {mask: partner(mask) for mask in range(1, grid)}
    core = lax.rem(here, 2)

    def ordered():
        chips = list(range(1, grid // 2))
        swapped = list(chips)
        if len(chips) >= 2:
            swapped[0], swapped[1] = chips[1], chips[0]
        for first, second in zip(chips, swapped):
            for bit in range(2):
                one, two = 2 * first + bit, 2 * second + bit
                yield one, two
        yield 1, 1

    order = []
    for one, two in ordered():
        order.append(partners[one] if one == two else partners[one] + core * (partners[two] - partners[one]))

    def storey(distance):
        return lax.rem(layer + distance, layers)

    def remote(source, target, sent, received, device):
        return pltpu.make_async_remote_copy(
            src_ref=source, dst_ref=target, send_sem=sent, recv_sem=received,
            device_id=device, device_id_type=pl.DeviceIdType.MESH,
        )

    def field_part(ref, group, device):
        first = (lax.rem(device, share) * own + group * orbs) * per
        return ref.at[:, lax.div(device, share), pl.ds(pl.multiple_of(first, 8), piece), :]

    def all_bytes(ref, sem):
        pltpu.make_async_copy(ref, ref, sem).wait()

    def signal(semaphore, device):
        pl.semaphore_signal(semaphore, inc=1, device_id=device, device_id_type=pl.DeviceIdType.MESH)

    for copy in loads:
        copy.start()
    for distance in range(1, layers):
        signal(barrier, (storey(distance), here))
    for other in partners.values():
        signal(barrier, (layer, other))

    def own_in(group):
        return pltpu.make_async_copy(field_part(field_ref, group, here), land_ref.at[group, here], in_recv.at[group])

    def own_out(group):
        return pltpu.make_async_copy(land_ref.at[group, here], field_part(out_ref, group, here), out_recv.at[group])

    def own_side():
        return pltpu.make_async_copy(packed_ref.at[here], side_ref.at[here], side_recv)

    for group in range(groups):
        own_in(group).start()
    for copy in loads:
        copy.wait()
    limit = jnp.where(material_ref[me] == 1, share * own, share * own // 2) - lax.rem(here, share) * own
    my_cell, my_kind = cell_ref[me], kind_ref[me]
    for target in range(grid):
        kind = kind_ref[layer * points + target // share]
        chosen = jnp.zeros(projector_ref.shape[1:], F32)
        for number in range(kinds):
            chosen = jnp.where(kind == number, projector_ref[number], chosen)
        packed_ref[target, :nproj * per] = chosen
        packed_ref[target, nproj * per:nproj * per + per] = potential_ref[target // share]
        spare = packed_ref.shape[1] - nproj * per - per
        if spare:
            packed_ref[target, nproj * per + per:] = jnp.zeros((spare, lanes), F32)
    own_side().start()
    pl.semaphore_wait(barrier, grid + layers - 2)
    for other in order:
        remote(packed_ref.at[other], side_ref.at[here], side_send, side_recv, (layer, other)).start()
    for group in range(groups):
        for other in order:
            remote(
                field_part(field_ref, group, other), land_ref.at[group, here],
                in_send.at[group], in_recv.at[group], (layer, other),
            ).start()

    for distance in range(1, layers):
        signal(ready_sem, (storey(distance), here))
    for line, rows in ((line_now_ref, vector_ref), (line_old_ref, previous_ref)):
        rows[...] = jnp.zeros(rows.shape, F32)
        for top in range(0, macro, LANES):
            length = min(LANES, macro - top)
            rows[top // LANES, :length] = line[pl.ds(top, length)]
    lane = lax.broadcasted_iota(jnp.int32, (1, lanes), 1)
    block_of = lax.rem(lane, lanes // 2) // orbs
    orbital_of = lax.rem(lane, orbs)
    sign = jnp.where(lane < lanes // 2, 1.0, -1.0).astype(F32)
    place = lax.rem(lane, lanes // 2)

    def turn(value, count):
        if blocks == 1:
            return value
        shift = count % blocks * orbs
        return jnp.where(place >= shift, pltpu.roll(value, shift, 1), pltpu.roll(value, lanes // 2 + shift, 1))

    weight = jnp.where(my_kind == 0, strength_ref[0:1, :], 0.0)
    for number in range(1, kinds):
        weight = weight + jnp.where(my_kind == number, strength_ref[number:number + 1, :], 0.0)
    weight = jnp.broadcast_to(weight * (2.0 * SPACING**2), (nproj, nproj))
    eye = lax.broadcasted_iota(jnp.int32, (nproj, nproj), 0) == lax.broadcasted_iota(jnp.int32, (nproj, nproj), 1)
    weight_ref[...] = jnp.broadcast_to(jnp.sum(jnp.where(eye, weight, 0.0), axis=1, keepdims=True), (nproj, lanes))

    all_bytes(side_ref, side_recv)

    def parted(ref, top):
        return ref[pl.ds(top, NZ // 2, stride=2), :], ref[pl.ds(top + 1, NZ // 2, stride=2), :]

    def columns(rows, spare):
        tall = rows.T
        for part in range(tall.shape[1] // lanes):
            spare[part] = tall[:, part * lanes:(part + 1) * lanes]
        return jnp.concatenate(
            [
                jnp.concatenate(
                    [piece for y in range(lanes // NZ) for piece in parted(spare.at[part], y * NZ)], axis=0
                )
                for part in range(tall.shape[1] // lanes)
            ],
            axis=1,
        )

    def prepare(slot, carry):
        for half in range(wide):
            level, highs, lows = [], [], []
            for block in range(blocks):
                x = block * slots + slot
                owner, plane = lax.div(x, mine), lax.rem(x, mine)
                row = half * mine + plane
                high, low = halves(side_ref[owner, pl.ds(row, nproj, stride=per), :])
                highs.append(high.astype(F32))
                lows.append(low.astype(F32))
                level.append(jnp.broadcast_to(side_ref[owner, pl.ds(nproj * per + row, 1), :], (orbs, lanes)))
            cells_here = pl.ds(pl.multiple_of(slot * cells + half * lanes, lanes), lanes)
            for number, part in enumerate((highs, lows)):
                tall = columns(jnp.concatenate(part, axis=0), spare_ref.at[number])
                fore_ref[number * width:(number + 1) * width, cells_here] = tall.T.astype(BF16)
                tall = tall.astype(BF16)
                back_ref[cells_here, number * width:(number + 1) * width] = tall
            diag_ref[cells_here, :] = columns(jnp.concatenate(level * 2, axis=0), spare_ref.at[2]) * (2.0 * SPACING**2)
        return carry

    lax.fori_loop(0, slots, prepare, 0)

    def store(term, slot, rows, value):
        terms[term][slot + 1, rows, :] = value
        if slot == 0:
            terms[term][slots + 1, rows, :] = turn(value, blocks - 1)
        if slot == slots - 1:
            terms[term][0, rows, :] = turn(value, 1)

    def setup(group):
        for slot in range(slots):
            for half in range(wide):
                pieces = []
                for part in range(2):
                    for block in range(blocks):
                        owner, plane = divmod(block * slots + slot, mine)
                        pieces.append(land_ref[group, owner, part, pl.ds(half * mine + plane, orbs, stride=per), :])
                spare = turned_ref.at[slot * wide + half]
                spare[...] = jnp.concatenate(pieces, axis=0).T
                for y in range(lanes // NZ):
                    top = half * lanes + y * NZ
                    for number, piece in enumerate(parted(spare, y * NZ)):
                        store(0, slot, slice(top + number * 8, top + number * 8 + 8), piece)

    def begin(group, planes_of):
        total = jnp.zeros((2 * width, 2 * lanes), F32)
        for slot in range(slots):
            high, low = halves(planes_of(slot))
            pieces = jnp.concatenate([high, low], axis=1)
            total = total + jnp.dot(fore_ref[:, slot * cells:(slot + 1) * cells], pieces, preferred_element_type=F32)
        total = total[:, :lanes] + total[:, lanes:]
        start_ref[group] = distant(total[:width] + total[width:])

    def distant(total):
        both = jnp.dot(back_ref[...], spread(total), preferred_element_type=F32)
        return both[:, :lanes] + both[:, lanes:]

    def restore(group):
        for slot in range(slots):
            for top in range(0, cells, NZ):
                store(0, slot, slice(top, top + NZ), keep_ref[group, slot, top:top + NZ, :])

    def finish(group):
        occupied = jnp.where(orbital_of + group * orbs < limit, 1.0, 0.0)
        for slot in range(slots):
            for half in range(wide):
                spare = turned_ref.at[slot * wide + half]
                for y in range(lanes // NZ):
                    top = half * lanes + y * NZ
                    for number in range(2):
                        spare[pl.ds(y * NZ + number, 8, stride=2), :] = (
                            keep_ref[group, slot, top + number * 8:top + number * 8 + 8, :] * occupied
                        )
                value = spare[...].T
                for part in range(2):
                    for block in range(blocks):
                        owner, plane = divmod(block * slots + slot, mine)
                        top = (part * blocks + block) * orbs
                        land_ref[group, owner, part, pl.ds(half * mine + plane, orbs, stride=per), :] = value[top:top + orbs]

    def spread(total):
        c = jnp.zeros((nproj, lanes), F32)
        for block in range(blocks):
            c = c + jnp.where(block_of == block, total[block * nproj:(block + 1) * nproj], 0.0)
        summed = c
        for count in range(1, blocks):
            summed = summed + turn(c, count)
        summed = summed * weight_ref[...]
        high, low = halves(jnp.concatenate([jnp.where(block_of == block, summed, 0.0) for block in range(blocks)], axis=0))
        both = jnp.concatenate([high, low], axis=1)
        return jnp.concatenate([both, both], axis=0)

    def degrees(group, a):
        flow, density = jnp.zeros((8, lanes), F32), jnp.zeros((8, lanes), F32)
        total = None
        lines = cells // NZ
        for degree in range(1, ORDER + 1):
            scale = TIME_STEP / degree
            swap_scale = sign * (scale / (2.0 * SPACING**2))
            drift_scale = a * (scale / (2.0 * SPACING))
            source = terms[degree - 1]
            final = degree == ORDER
            if degree > 1:
                nonlocal_ref[degree - 2] = distant(total)
            far = start_ref.at[group] if degree == 1 else nonlocal_ref.at[degree - 2]
            for slot in range(slots):
                for y in range(lines):
                    tops = (y * NZ, y * NZ + 8)
                    up, down = (y + 1) % lines * NZ, (y - 1) % lines * NZ
                    even, odd = (source[slot + 1, top:top + 8, :] for top in tops)
                    after, before = pltpu.roll(even, 7, 0), pltpu.roll(odd, 1, 0)
                    fresh = []
                    for number, (value, ahead, behind) in enumerate(((even, odd, before), (odd, after, even))):
                        rows = slice(tops[number], tops[number] + 8)
                        beside = (ahead + behind) + (
                            source[slot + 1, up + number * 8:up + number * 8 + 8, :]
                            + source[slot + 1, down + number * 8:down + number * 8 + 8, :]
                        ) + (source[slot, rows, :] + source[slot + 2, rows, :])
                        flat_rows = slice(slot * cells + rows.start, slot * cells + rows.stop)
                        level = level_ref[flat_rows, :] * value - beside + far[flat_rows, :]
                        new = swap_scale * pltpu.roll(level, lanes // 2, 1) - drift_scale * (ahead - behind)
                        if final:
                            new = new + value
                            for term in terms[:ORDER - 1]:
                                new = new + term[slot + 1, rows, :]
                            keep_ref[group, slot, rows, :] = new
                        else:
                            store(degree, slot, rows, new)
                        fresh.append(new)
                    if final:
                        even, odd = fresh
                        for value, slope in ((even, odd - pltpu.roll(odd, 1, 0)), (odd, pltpu.roll(even, 7, 0) - even)):
                            flow = flow + value * pltpu.roll(slope, lanes // 2, 1)
                            density = density + value * value
                    else:
                        top = slot * cells + y * NZ
                        parts_ref[degree - 1, top:top + NZ, :] = jnp.concatenate(fresh, axis=0).astype(BF16)
                last = slots * cells - cells
                if not final and slot == slots - 2:
                    total = jnp.dot(fore_ref[:width, :last], parts_ref[degree - 1, :last, :], preferred_element_type=F32)
                if not final and slot == slots - 1:
                    total = total + jnp.dot(fore_ref[:width, last:], parts_ref[degree - 1, last:, :], preferred_element_type=F32)
        flow_ref[0] = flow_ref[0] + flow * jnp.where(orbital_of + group * orbs < limit, sign * (0.5 / SPACING), 0.0)
        flow_ref[1] = flow_ref[1] + density * jnp.where(orbital_of + group * orbs < limit, 1.0, 0.0)

    flat = (
        lax.broadcasted_iota(jnp.int32, vector_ref.shape, 0) * vector_ref.shape[1]
        + lax.broadcasted_iota(jnp.int32, vector_ref.shape, 1)
    )

    def send_back(group):
        for other in order:
            remote(
                land_ref.at[group, other], field_part(out_ref, group, here),
                out_send.at[group], out_recv.at[group], (layer, other),
            ).start()
        own_out(group).start()

    def advance(step, a):
        base = 6.0 + (SPACING * SPACING) * a * a
        level_ref[...] = diag_ref[...] + base
        flow_ref[...] = jnp.zeros(flow_ref.shape, F32)

        def advance_group(group, carry):
            @pl.when(step == 0)
            def _():
                all_bytes(land_ref.at[group], in_recv.at[group])
                setup(group)
                begin(group, lambda slot: first_ref[slot + 1])

            @pl.when(step * group > 0)
            def _():
                restore(group)

            degrees(group, a)

            @pl.when(step == STEPS - 1)
            def _():
                finish(group)

                @pl.when(group < groups - 1)
                def _():
                    send_back(group)

            return carry

        lax.fori_loop(0, groups, advance_group, 0)
        row_ref[step] = jnp.full((1, LANES), jnp.sum(flow_ref[0] + a * flow_ref[1]) * norm, F32)
        mine_row = pltpu.make_async_copy(row_ref.at[step], rows_ref.at[step, layer * grid + here], row_recv.at[step])
        mine_row.start()

        @pl.when(step == 0)
        def _():
            pl.semaphore_wait(ready_sem, layers - 1)

        for distance in range(layers - 1, -1, -1):
            for mask in range(grid):
                if distance > 0 or mask > 0:
                    other = partners[mask] if mask else here
                    remote(
                        row_ref.at[step], rows_ref.at[step, layer * grid + here],
                        row_send.at[step], row_recv.at[step], (storey(distance), other),
                    ).start()

        @pl.when(step == STEPS - 1)
        def _():
            send_back(groups - 1)

        @pl.when(step == 0)
        def _():
            def again(group, carry):
                begin(group, lambda slot: keep_ref[group, slot])
                return carry

            lax.fori_loop(0, groups, again, 0)
            restore(0)

        present = vector_ref[...]
        following = macro_update(present, previous_ref[...], macro)
        own_following = jnp.sum(jnp.where(flat == my_cell, following, 0.0))
        for floor in range(layers):
            for member in range(grid):
                same = cell_ref[floor * points + member // share] == my_cell
                mask_ref[floor * grid + member] = jnp.full((1, LANES), jnp.where(same, COUPLING / LANES, 0.0), F32)
        all_bytes(rows_ref.at[step], row_recv.at[step])
        own_deposit = jnp.sum(rows_ref[step] * mask_ref[...])
        deposit = jnp.zeros(flat.shape, F32)
        for floor in range(layers):
            for member in range(grid):
                cell = cell_ref[floor * points + member // share]
                deposit = deposit + jnp.where(flat == cell, rows_ref[step, floor * grid + member], 0.0)
        vector_ref[...] = following - COUPLING * deposit
        previous_ref[...] = present
        return own_following - own_deposit

    lax.fori_loop(0, STEPS, advance, jnp.sum(jnp.where(flat == my_cell, vector_ref[...], 0.0)))
    all_bytes(packed_ref.at[pl.ds(0, grid - 1)], side_send)
    for step in range(STEPS):
        all_bytes(rows_ref.at[step, pl.ds(0, grid * layers - 1)], row_send.at[step])
    for group in range(groups):
        all_bytes(land_ref.at[group, pl.ds(0, grid - 1)], in_send.at[group])
        all_bytes(land_ref.at[group, pl.ds(0, grid - 1)], out_send.at[group])
        all_bytes(land_ref.at[group], out_recv.at[group])


def propagate(materials, kinds, owners, strengths, projectors, potential, field, now, old, norm, macro, share, grid, layers, mine, own):
    points, per, lanes = potential.shape
    cells = per // mine * lanes
    planes = grid * mine
    orbs = own // GROUPS
    blocks = lanes // (2 * orbs)
    slots = planes // blocks
    nproj = strengths.shape[1]
    rows = nproj * per
    tall = rows + -(-per // 8) * 8
    vmem = pl.BlockSpec(memory_space=pltpu.VMEM)
    hbm = pl.BlockSpec(memory_space=pltpu.HBM)
    dma = lambda *shape: pltpu.SemaphoreType.DMA(shape)
    return pl.pallas_call(
        functools.partial(kernel, norm, macro, share, grid, layers, mine, own),
        out_shape=(
            jax.ShapeDtypeStruct(field.shape, F32),
            jax.ShapeDtypeStruct((-(-macro // 1024) * 8, LANES), F32),
        ),
        in_specs=[hbm] * 9,
        out_specs=(hbm, vmem),
        scratch_shapes=[
            pltpu.SMEM(materials.shape, jnp.int32),
            pltpu.SMEM(kinds.shape, jnp.int32),
            pltpu.SMEM(owners.shape, jnp.int32),
            pltpu.VMEM(strengths.shape, F32),
            pltpu.VMEM(projectors.shape, F32),
            pltpu.VMEM(potential.shape, F32),
            *[pltpu.VMEM((slots + 2, cells, lanes), F32)] * ORDER,
            pltpu.VMEM((GROUPS, slots, cells, lanes), F32),
            pltpu.VMEM((GROUPS, grid, 2, orbs * per, lanes), F32),
            pltpu.VMEM((ORDER - 1, slots * cells, lanes), BF16),
            pltpu.VMEM((GROUPS, slots * cells, lanes), F32),
            pltpu.VMEM((grid, tall, lanes), F32),
            pltpu.VMEM((grid, tall, lanes), F32),
            pltpu.VMEM((2 * blocks * nproj, slots * cells), BF16),
            pltpu.VMEM((slots * cells, 2 * blocks * nproj), BF16),
            pltpu.VMEM((slots * cells, lanes), F32),
            pltpu.VMEM((slots * cells, lanes), F32),
            pltpu.VMEM((nproj, lanes), F32),
            pltpu.VMEM((-(-macro // 1024) * 8, LANES), F32),
            pltpu.VMEM(now.shape, F32),
            pltpu.VMEM(old.shape, F32),
            pltpu.VMEM((STEPS, 1, LANES), F32),
            pltpu.VMEM((STEPS, layers * grid, 1, LANES), F32),
            pltpu.VMEM((2, 8, lanes), F32),
            pltpu.VMEM((3, blocks * nproj // lanes, lanes, lanes), F32),
            pltpu.VMEM((planes // blocks * (cells // lanes), lanes, lanes), F32),
            pltpu.VMEM((ORDER - 1, slots * cells, lanes), F32),
            pltpu.VMEM((layers * grid, 1, LANES), F32),
            dma(GROUPS), dma(GROUPS),
            pltpu.SemaphoreType.DMA, pltpu.SemaphoreType.DMA,
            dma(GROUPS), dma(GROUPS),
            dma(STEPS), dma(STEPS),
            dma(8),
            pltpu.SemaphoreType.REGULAR,
        ],
        compiler_params=pltpu.CompilerParams(
            vmem_limit_bytes=48 * 1024 * 1024, collective_id=0, has_side_effects=True
        ),
        name="propagate",
    )(materials, kinds, owners, strengths, projectors, potential, field, now, old)


def rows_of(array, lanes=LANES):
    lead, (planes, cells) = array.shape[:-2], array.shape[-2:]
    array = array.reshape(lead + (planes, cells // lanes, lanes))
    return jnp.swapaxes(array, -3, -2).reshape(lead + (planes * cells // lanes, lanes))


def local(
    orbitals, local_potential, projectors, strengths, material, proj_kind, point_cell,
    vector_now, vector_old, grid, layers,
):
    _, points, orb, mine, cells = orbitals.shape
    assert grid % points == 0 and orb % (grid // points) == 0
    share = grid // points
    own = orb // share
    wide = cells // LANES
    per = wide * mine
    kinds, nproj = strengths.shape
    macro = vector_now.shape[0]
    held = lambda array: pltpu.with_memory_space_constraint(array, pltpu.HBM)
    field, vector = propagate(
        held(material), held(proj_kind), held(point_cell), held(strengths),
        held(rows_of(projectors).reshape(kinds, nproj * per, LANES)),
        held(rows_of(local_potential)),
        held(rows_of(orbitals).reshape(2, points, orb * per, LANES)),
        held(vector_now), held(vector_old),
        2.0 / (orb * grid * mine * cells), macro, share, grid, layers, mine, own,
    )
    field = jnp.swapaxes(field.reshape(2, points, orb, wide, mine, LANES), -3, -2).reshape(orbitals.shape)
    return field, vector.reshape(-1)[:macro]


def solution(mesh):
    in_specs = (
        P(None, "micro", None, "grid", None),
        P("micro", "grid", None),
        P(None, None, "grid", None),
        P(),
        P(),
        P(),
        P(),
        P(),
        P(),
    )
    out_specs = (P(None, "micro", None, "grid", None), P())
    body = functools.partial(local, grid=mesh.shape["grid"], layers=mesh.shape["micro"])
    return jax.shard_map(body, mesh=mesh, in_specs=in_specs, out_specs=out_specs, check_vma=False)
```

```python
import functools

import jax
import jax.numpy as jnp
from jax import lax
from jax.experimental import pallas as pl
from jax.experimental.pallas import tpu as pltpu
from jax.sharding import PartitionSpec as P

NZ = 16
STEPS = 2
ORDER = 4
LANES = 128
GROUPS = 4

SPACING = 0.64
TIME_STEP = 0.05
COURANT = 0.9
COUPLING = 1.0
F32 = jnp.float32
BF16 = jnp.bfloat16


def halves(value):
    high = value.astype(BF16)
    return high, (value - high.astype(F32)).astype(BF16)


def macro_update(present, previous, macro):
    high, lanes = present.shape
    lane = lax.broadcasted_iota(jnp.int32, present.shape, 1)
    flat = lax.broadcasted_iota(jnp.int32, present.shape, 0) * lanes + lane
    ahead = pltpu.roll(present, lanes - 1, 1)
    ahead = jnp.where(lane == lanes - 1, pltpu.roll(ahead, high - 1, 0), ahead)
    behind = pltpu.roll(present, 1, 1)
    behind = jnp.where(lane == 0, pltpu.roll(behind, 1, 0), behind)
    curvature = ahead + behind - 2.0 * present
    following = 2.0 * present - previous + COURANT**2 * curvature
    return jnp.where(flat < macro, following, 0.0)


def kernel(
    norm, macro, share, grid, layers, mine, own,
    material_in, kind_in, cell_in, strength_in, projector_in, potential_in, field_ref, now_in, old_in,
    out_ref, vector_ref,
    material_ref, kind_ref, cell_ref, strength_ref, projector_ref, potential_ref,
    first_ref, second_ref, third_ref, fourth_ref, keep_ref, land_ref, parts_ref, start_ref, packed_ref, side_ref, fore_ref, back_ref, diag_ref, level_ref, weight_ref,
    previous_ref, line_now_ref, line_old_ref, row_ref, rows_ref, flow_ref, spare_ref, turned_ref, nonlocal_ref, mask_ref,
    in_send, in_recv, side_send, side_recv, out_send, out_recv, row_send, row_recv, load_sem, ready_sem,
):
    groups, slots, cells, lanes = keep_ref.shape
    terms = (first_ref, second_ref, third_ref, fourth_ref)
    kinds, nproj = strength_ref.shape
    points, per, _ = potential_ref.shape
    wide = cells // lanes
    orbs = own // groups
    blocks = lanes // (2 * orbs)
    here = lax.axis_index("grid")
    layer = lax.axis_index("micro")
    me = layer * points + lax.div(here, share)
    piece = orbs * per
    width = blocks * nproj
    barrier = pltpu.get_barrier_semaphore()

    loads = [
        pltpu.make_async_copy(source, target, load_sem.at[number])
        for number, (source, target) in enumerate((
            (material_in, material_ref), (kind_in, kind_ref), (cell_in, cell_ref),
            (strength_in, strength_ref), (projector_in, projector_ref), (potential_in, potential_ref),
            (now_in, line_now_ref), (old_in, line_old_ref),
        ))
    ]

    def partner(mask):
        other, bit = 0, 1
        while bit < grid:
            own_bit = lax.rem(lax.div(here, bit), 2)
            other = other + (1 - own_bit if mask & bit else own_bit) * bit
            bit *= 2
        return other

    partners = {mask: partner(mask) for mask in range(1, grid)}
    core = lax.rem(here, 2)

    def ordered():
        chips = list(range(1, grid // 2))
        swapped = list(chips)
        if len(chips) >= 2:
            swapped[0], swapped[1] = chips[1], chips[0]
        for first, second in zip(chips, swapped):
            for bit in range(2):
                one, two = 2 * first + bit, 2 * second + bit
                yield one, two
        yield 1, 1

    order = []
    for one, two in ordered():
        order.append(partners[one] if one == two else partners[one] + core * (partners[two] - partners[one]))

    def storey(distance):
        return lax.rem(layer + distance, layers)

    def remote(source, target, sent, received, device):
        return pltpu.make_async_remote_copy(
            src_ref=source, dst_ref=target, send_sem=sent, recv_sem=received,
            device_id=device, device_id_type=pl.DeviceIdType.MESH,
        )

    def field_part(ref, group, device):
        first = (lax.rem(device, share) * own + group * orbs) * per
        return ref.at[:, lax.div(device, share), pl.ds(pl.multiple_of(first, 8), piece), :]

    def all_bytes(ref, sem):
        pltpu.make_async_copy(ref, ref, sem).wait()

    def signal(semaphore, device):
        pl.semaphore_signal(semaphore, inc=1, device_id=device, device_id_type=pl.DeviceIdType.MESH)

    for copy in loads:
        copy.start()
    for distance in range(1, layers):
        signal(barrier, (storey(distance), here))
    for other in partners.values():
        signal(barrier, (layer, other))

    def own_in(group):
        return pltpu.make_async_copy(field_part(field_ref, group, here), land_ref.at[group, here], in_recv.at[group])

    def own_out(group):
        return pltpu.make_async_copy(land_ref.at[group, here], field_part(out_ref, group, here), out_recv.at[group])

    def own_side():
        return pltpu.make_async_copy(packed_ref.at[here], side_ref.at[here], side_recv)

    for group in range(groups):
        own_in(group).start()
    for copy in loads:
        copy.wait()
    limit = jnp.where(material_ref[me] == 1, share * own, share * own // 2) - lax.rem(here, share) * own
    my_cell, my_kind = cell_ref[me], kind_ref[me]
    for target in range(grid):
        kind = kind_ref[layer * points + target // share]
        chosen = jnp.zeros(projector_ref.shape[1:], F32)
        for number in range(kinds):
            chosen = jnp.where(kind == number, projector_ref[number], chosen)
        packed_ref[target, :nproj * per] = chosen
        packed_ref[target, nproj * per:nproj * per + per] = potential_ref[target // share]
        spare = packed_ref.shape[1] - nproj * per - per
        if spare:
            packed_ref[target, nproj * per + per:] = jnp.zeros((spare, lanes), F32)
    own_side().start()
    pl.semaphore_wait(barrier, grid + layers - 2)
    for other in order:
        remote(packed_ref.at[other], side_ref.at[here], side_send, side_recv, (layer, other)).start()
    for group in range(groups):
        for other in order:
            remote(
                field_part(field_ref, group, other), land_ref.at[group, here],
                in_send.at[group], in_recv.at[group], (layer, other),
            ).start()

    for distance in range(1, layers):
        signal(ready_sem, (storey(distance), here))
    for line, rows in ((line_now_ref, vector_ref), (line_old_ref, previous_ref)):
        rows[...] = jnp.zeros(rows.shape, F32)
        for top in range(0, macro, LANES):
            length = min(LANES, macro - top)
            rows[top // LANES, :length] = line[pl.ds(top, length)]
    lane = lax.broadcasted_iota(jnp.int32, (1, lanes), 1)
    block_of = lax.rem(lane, lanes // 2) // orbs
    orbital_of = lax.rem(lane, orbs)
    sign = jnp.where(lane < lanes // 2, 1.0, -1.0).astype(F32)
    place = lax.rem(lane, lanes // 2)

    def turn(value, count):
        if blocks == 1:
            return value
        shift = count % blocks * orbs
        return jnp.where(place >= shift, pltpu.roll(value, shift, 1), pltpu.roll(value, lanes // 2 + shift, 1))

    weight = jnp.where(my_kind == 0, strength_ref[0:1, :], 0.0)
    for number in range(1, kinds):
        weight = weight + jnp.where(my_kind == number, strength_ref[number:number + 1, :], 0.0)
    weight = jnp.broadcast_to(weight * (2.0 * SPACING**2), (nproj, nproj))
    eye = lax.broadcasted_iota(jnp.int32, (nproj, nproj), 0) == lax.broadcasted_iota(jnp.int32, (nproj, nproj), 1)
    weight_ref[...] = jnp.broadcast_to(jnp.sum(jnp.where(eye, weight, 0.0), axis=1, keepdims=True), (nproj, lanes))

    all_bytes(side_ref, side_recv)

    def parted(ref, top):
        return ref[pl.ds(top, NZ // 2, stride=2), :], ref[pl.ds(top + 1, NZ // 2, stride=2), :]

    def columns(rows, spare):
        tall = rows.T
        for part in range(tall.shape[1] // lanes):
            spare[part] = tall[:, part * lanes:(part + 1) * lanes]
        return jnp.concatenate(
            [
                jnp.concatenate(
                    [piece for y in range(lanes // NZ) for piece in parted(spare.at[part], y * NZ)], axis=0
                )
                for part in range(tall.shape[1] // lanes)
            ],
            axis=1,
        )

    def prepare(slot, carry):
        for half in range(wide):
            level, highs, lows = [], [], []
            for block in range(blocks):
                x = block * slots + slot
                owner, plane = lax.div(x, mine), lax.rem(x, mine)
                row = half * mine + plane
                high, low = halves(side_ref[owner, pl.ds(row, nproj, stride=per), :])
                highs.append(high.astype(F32))
                lows.append(low.astype(F32))
                level.append(jnp.broadcast_to(side_ref[owner, pl.ds(nproj * per + row, 1), :], (orbs, lanes)))
            cells_here = pl.ds(pl.multiple_of(slot * cells + half * lanes, lanes), lanes)
            for number, part in enumerate((highs, lows)):
                tall = columns(jnp.concatenate(part, axis=0), spare_ref.at[number])
                fore_ref[number * width:(number + 1) * width, cells_here] = tall.T.astype(BF16)
                tall = tall.astype(BF16)
                back_ref[cells_here, number * width:(number + 1) * width] = tall
            diag_ref[cells_here, :] = columns(jnp.concatenate(level * 2, axis=0), spare_ref.at[2]) * (2.0 * SPACING**2)
        return carry

    lax.fori_loop(0, slots, prepare, 0)

    def store(term, slot, rows, value):
        terms[term][slot + 1, rows, :] = value
        if slot == 0:
            terms[term][slots + 1, rows, :] = turn(value, blocks - 1)
        if slot == slots - 1:
            terms[term][0, rows, :] = turn(value, 1)

    def setup(group):
        for slot in range(slots):
            for half in range(wide):
                pieces = []
                for part in range(2):
                    for block in range(blocks):
                        owner, plane = divmod(block * slots + slot, mine)
                        pieces.append(land_ref[group, owner, part, pl.ds(half * mine + plane, orbs, stride=per), :])
                spare = turned_ref.at[slot * wide + half]
                spare[...] = jnp.concatenate(pieces, axis=0).T
                for y in range(lanes // NZ):
                    top = half * lanes + y * NZ
                    for number, piece in enumerate(parted(spare, y * NZ)):
                        store(0, slot, slice(top + number * 8, top + number * 8 + 8), piece)

    def begin(group, planes_of):
        total = jnp.zeros((2 * width, 2 * lanes), F32)
        for slot in range(slots):
            high, low = halves(planes_of(slot))
            pieces = jnp.concatenate([high, low], axis=1)
            total = total + jnp.dot(fore_ref[:, slot * cells:(slot + 1) * cells], pieces, preferred_element_type=F32)
        total = total[:, :lanes] + total[:, lanes:]
        start_ref[group] = distant(total[:width] + total[width:])

    def distant(total):
        both = jnp.dot(back_ref[...], spread(total), preferred_element_type=F32)
        return both[:, :lanes] + both[:, lanes:]

    def restore(group):
        for slot in range(slots):
            for top in range(0, cells, NZ):
                store(0, slot, slice(top, top + NZ), keep_ref[group, slot, top:top + NZ, :])

    def finish(group):
        occupied = jnp.where(orbital_of + group * orbs < limit, 1.0, 0.0)
        for slot in range(slots):
            for half in range(wide):
                spare = turned_ref.at[slot * wide + half]
                for y in range(lanes // NZ):
                    top = half * lanes + y * NZ
                    for number in range(2):
                        spare[pl.ds(y * NZ + number, 8, stride=2), :] = (
                            keep_ref[group, slot, top + number * 8:top + number * 8 + 8, :] * occupied
                        )
                value = spare[...].T
                for part in range(2):
                    for block in range(blocks):
                        owner, plane = divmod(block * slots + slot, mine)
                        top = (part * blocks + block) * orbs
                        land_ref[group, owner, part, pl.ds(half * mine + plane, orbs, stride=per), :] = value[top:top + orbs]

    def spread(total):
        c = jnp.zeros((nproj, lanes), F32)
        for block in range(blocks):
            c = c + jnp.where(block_of == block, total[block * nproj:(block + 1) * nproj], 0.0)
        summed = c
        for count in range(1, blocks):
            summed = summed + turn(c, count)
        summed = summed * weight_ref[...]
        high, low = halves(jnp.concatenate([jnp.where(block_of == block, summed, 0.0) for block in range(blocks)], axis=0))
        both = jnp.concatenate([high, low], axis=1)
        return jnp.concatenate([both, both], axis=0)

    def degrees(group, a):
        flow, density = jnp.zeros((8, lanes), F32), jnp.zeros((8, lanes), F32)
        total = None
        lines = cells // NZ
        for degree in range(1, ORDER + 1):
            scale = TIME_STEP / degree
            swap_scale = sign * (scale / (2.0 * SPACING**2))
            drift_scale = a * (scale / (2.0 * SPACING))
            source = terms[degree - 1]
            final = degree == ORDER
            if degree > 1:
                nonlocal_ref[degree - 2] = distant(total)
            far = start_ref.at[group] if degree == 1 else nonlocal_ref.at[degree - 2]
            for slot in range(slots):
                for y in range(lines):
                    tops = (y * NZ, y * NZ + 8)
                    up, down = (y + 1) % lines * NZ, (y - 1) % lines * NZ
                    even, odd = (source[slot + 1, top:top + 8, :] for top in tops)
                    after, before = pltpu.roll(even, 7, 0), pltpu.roll(odd, 1, 0)
                    fresh = []
                    for number, (value, ahead, behind) in enumerate(((even, odd, before), (odd, after, even))):
                        rows = slice(tops[number], tops[number] + 8)
                        beside = (ahead + behind) + (
                            source[slot + 1, up + number * 8:up + number * 8 + 8, :]
                            + source[slot + 1, down + number * 8:down + number * 8 + 8, :]
                        ) + (source[slot, rows, :] + source[slot + 2, rows, :])
                        flat_rows = slice(slot * cells + rows.start, slot * cells + rows.stop)
                        level = level_ref[flat_rows, :] * value - beside + far[flat_rows, :]
                        new = swap_scale * pltpu.roll(level, lanes // 2, 1) - drift_scale * (ahead - behind)
                        if final:
                            new = new + value
                            for term in terms[:ORDER - 1]:
                                new = new + term[slot + 1, rows, :]
                            keep_ref[group, slot, rows, :] = new
                        else:
                            store(degree, slot, rows, new)
                        fresh.append(new)
                    if final:
                        even, odd = fresh
                        for value, slope in ((even, odd - pltpu.roll(odd, 1, 0)), (odd, pltpu.roll(even, 7, 0) - even)):
                            flow = flow + value * pltpu.roll(slope, lanes // 2, 1)
                            density = density + value * value
                    else:
                        top = slot * cells + y * NZ
                        parts_ref[degree - 1, top:top + NZ, :] = jnp.concatenate(fresh, axis=0).astype(BF16)
                if not final and slot in (slots // 2 - 1, slots - 1):
                    first = 0 if slot < slots // 2 else slots // 2 * cells
                    here_cells = slice(first, (slot + 1) * cells)
                    part = jnp.dot(fore_ref[:width, here_cells], parts_ref[degree - 1, here_cells, :], preferred_element_type=F32)
                    total = part if first == 0 else total + part
        flow_ref[0] = flow_ref[0] + flow * jnp.where(orbital_of + group * orbs < limit, sign * (0.5 / SPACING), 0.0)
        flow_ref[1] = flow_ref[1] + density * jnp.where(orbital_of + group * orbs < limit, 1.0, 0.0)

    flat = (
        lax.broadcasted_iota(jnp.int32, vector_ref.shape, 0) * vector_ref.shape[1]
        + lax.broadcasted_iota(jnp.int32, vector_ref.shape, 1)
    )

    def send_back(group):
        for other in order:
            remote(
                land_ref.at[group, other], field_part(out_ref, group, here),
                out_send.at[group], out_recv.at[group], (layer, other),
            ).start()
        own_out(group).start()

    def advance(step, a):
        base = 6.0 + (SPACING * SPACING) * a * a
        level_ref[...] = diag_ref[...] + base
        flow_ref[...] = jnp.zeros(flow_ref.shape, F32)

        def advance_group(group, carry):
            @pl.when(step == 0)
            def _():
                all_bytes(land_ref.at[group], in_recv.at[group])
                setup(group)
                begin(group, lambda slot: first_ref[slot + 1])

            @pl.when(step * group > 0)
            def _():
                restore(group)

            degrees(group, a)

            @pl.when(step == STEPS - 1)
            def _():
                finish(group)

                @pl.when(group < groups - 1)
                def _():
                    send_back(group)

            return carry

        lax.fori_loop(0, groups, advance_group, 0)
        row_ref[step] = jnp.full((1, LANES), jnp.sum(flow_ref[0] + a * flow_ref[1]) * norm, F32)
        mine_row = pltpu.make_async_copy(row_ref.at[step], rows_ref.at[step, layer * grid + here], row_recv.at[step])
        mine_row.start()

        @pl.when(step == 0)
        def _():
            pl.semaphore_wait(ready_sem, layers - 1)

        for distance in range(layers - 1, -1, -1):
            for mask in range(grid):
                if distance > 0 or mask > 0:
                    other = partners[mask] if mask else here
                    remote(
                        row_ref.at[step], rows_ref.at[step, layer * grid + here],
                        row_send.at[step], row_recv.at[step], (storey(distance), other),
                    ).start()

        @pl.when(step == STEPS - 1)
        def _():
            send_back(groups - 1)

        @pl.when(step == 0)
        def _():
            def again(group, carry):
                begin(group, lambda slot: keep_ref[group, slot])
                return carry

            lax.fori_loop(0, groups, again, 0)
            restore(0)

        present = vector_ref[...]
        following = macro_update(present, previous_ref[...], macro)
        own_following = jnp.sum(jnp.where(flat == my_cell, following, 0.0))
        for floor in range(layers):
            for member in range(grid):
                same = cell_ref[floor * points + member // share] == my_cell
                mask_ref[floor * grid + member] = jnp.full((1, LANES), jnp.where(same, COUPLING / LANES, 0.0), F32)
        all_bytes(rows_ref.at[step], row_recv.at[step])
        own_deposit = jnp.sum(rows_ref[step] * mask_ref[...])
        deposit = jnp.zeros(flat.shape, F32)
        for floor in range(layers):
            for member in range(grid):
                cell = cell_ref[floor * points + member // share]
                deposit = deposit + jnp.where(flat == cell, rows_ref[step, floor * grid + member], 0.0)
        vector_ref[...] = following - COUPLING * deposit
        previous_ref[...] = present
        return own_following - own_deposit

    lax.fori_loop(0, STEPS, advance, jnp.sum(jnp.where(flat == my_cell, vector_ref[...], 0.0)))
    all_bytes(packed_ref.at[pl.ds(0, grid - 1)], side_send)
    for step in range(STEPS):
        all_bytes(rows_ref.at[step, pl.ds(0, grid * layers - 1)], row_send.at[step])
    for group in range(groups):
        all_bytes(land_ref.at[group, pl.ds(0, grid - 1)], in_send.at[group])
        all_bytes(land_ref.at[group, pl.ds(0, grid - 1)], out_send.at[group])
        all_bytes(land_ref.at[group], out_recv.at[group])


def propagate(materials, kinds, owners, strengths, projectors, potential, field, now, old, norm, macro, share, grid, layers, mine, own):
    points, per, lanes = potential.shape
    cells = per // mine * lanes
    planes = grid * mine
    orbs = own // GROUPS
    blocks = lanes // (2 * orbs)
    slots = planes // blocks
    nproj = strengths.shape[1]
    rows = nproj * per
    tall = rows + -(-per // 8) * 8
    vmem = pl.BlockSpec(memory_space=pltpu.VMEM)
    hbm = pl.BlockSpec(memory_space=pltpu.HBM)
    dma = lambda *shape: pltpu.SemaphoreType.DMA(shape)
    return pl.pallas_call(
        functools.partial(kernel, norm, macro, share, grid, layers, mine, own),
        out_shape=(
            jax.ShapeDtypeStruct(field.shape, F32),
            jax.ShapeDtypeStruct((-(-macro // 1024) * 8, LANES), F32),
        ),
        in_specs=[hbm] * 9,
        out_specs=(hbm, vmem),
        scratch_shapes=[
            pltpu.SMEM(materials.shape, jnp.int32),
            pltpu.SMEM(kinds.shape, jnp.int32),
            pltpu.SMEM(owners.shape, jnp.int32),
            pltpu.VMEM(strengths.shape, F32),
            pltpu.VMEM(projectors.shape, F32),
            pltpu.VMEM(potential.shape, F32),
            *[pltpu.VMEM((slots + 2, cells, lanes), F32)] * ORDER,
            pltpu.VMEM((GROUPS, slots, cells, lanes), F32),
            pltpu.VMEM((GROUPS, grid, 2, orbs * per, lanes), F32),
            pltpu.VMEM((ORDER - 1, slots * cells, lanes), BF16),
            pltpu.VMEM((GROUPS, slots * cells, lanes), F32),
            pltpu.VMEM((grid, tall, lanes), F32),
            pltpu.VMEM((grid, tall, lanes), F32),
            pltpu.VMEM((2 * blocks * nproj, slots * cells), BF16),
            pltpu.VMEM((slots * cells, 2 * blocks * nproj), BF16),
            pltpu.VMEM((slots * cells, lanes), F32),
            pltpu.VMEM((slots * cells, lanes), F32),
            pltpu.VMEM((nproj, lanes), F32),
            pltpu.VMEM((-(-macro // 1024) * 8, LANES), F32),
            pltpu.VMEM(now.shape, F32),
            pltpu.VMEM(old.shape, F32),
            pltpu.VMEM((STEPS, 1, LANES), F32),
            pltpu.VMEM((STEPS, layers * grid, 1, LANES), F32),
            pltpu.VMEM((2, 8, lanes), F32),
            pltpu.VMEM((3, blocks * nproj // lanes, lanes, lanes), F32),
            pltpu.VMEM((planes // blocks * (cells // lanes), lanes, lanes), F32),
            pltpu.VMEM((ORDER - 1, slots * cells, lanes), F32),
            pltpu.VMEM((layers * grid, 1, LANES), F32),
            dma(GROUPS), dma(GROUPS),
            pltpu.SemaphoreType.DMA, pltpu.SemaphoreType.DMA,
            dma(GROUPS), dma(GROUPS),
            dma(STEPS), dma(STEPS),
            dma(8),
            pltpu.SemaphoreType.REGULAR,
        ],
        compiler_params=pltpu.CompilerParams(
            vmem_limit_bytes=48 * 1024 * 1024, collective_id=0, has_side_effects=True
        ),
        name="propagate",
    )(materials, kinds, owners, strengths, projectors, potential, field, now, old)


def rows_of(array, lanes=LANES):
    lead, (planes, cells) = array.shape[:-2], array.shape[-2:]
    array = array.reshape(lead + (planes, cells // lanes, lanes))
    return jnp.swapaxes(array, -3, -2).reshape(lead + (planes * cells // lanes, lanes))


def local(
    orbitals, local_potential, projectors, strengths, material, proj_kind, point_cell,
    vector_now, vector_old, grid, layers,
):
    _, points, orb, mine, cells = orbitals.shape
    assert grid % points == 0 and orb % (grid // points) == 0
    share = grid // points
    own = orb // share
    wide = cells // LANES
    per = wide * mine
    kinds, nproj = strengths.shape
    macro = vector_now.shape[0]
    held = lambda array: pltpu.with_memory_space_constraint(array, pltpu.HBM)
    field, vector = propagate(
        held(material), held(proj_kind), held(point_cell), held(strengths),
        held(rows_of(projectors).reshape(kinds, nproj * per, LANES)),
        held(rows_of(local_potential)),
        held(rows_of(orbitals).reshape(2, points, orb * per, LANES)),
        held(vector_now), held(vector_old),
        2.0 / (orb * grid * mine * cells), macro, share, grid, layers, mine, own,
    )
    field = jnp.swapaxes(field.reshape(2, points, orb, wide, mine, LANES), -3, -2).reshape(orbitals.shape)
    return field, vector.reshape(-1)[:macro]


def solution(mesh):
    in_specs = (
        P(None, "micro", None, "grid", None),
        P("micro", "grid", None),
        P(None, None, "grid", None),
        P(),
        P(),
        P(),
        P(),
        P(),
        P(),
    )
    out_specs = (P(None, "micro", None, "grid", None), P())
    body = functools.partial(local, grid=mesh.shape["grid"], layers=mesh.shape["micro"])
    return jax.shard_map(body, mesh=mesh, in_specs=in_specs, out_specs=out_specs, check_vma=False)
```
